32 devices in a mesh: parts: 2 (over x), slab: 8 (over z, y), freq: 2 (over core).
Axes of the slice: x: 2, y: 2, z: 4, core: 2. Of those that a mesh axis runs over, the one named last changes fastest.
Arguments:
- reflectivity: float32 [65536], P(('parts', 'slab')), parts along dimension 0, may hold values from -6 to 6
- source_green: bfloat16 [4, 65536, 2, 256], P('freq', ('parts', 'slab')), parts along dimension 1, may hold values from -6 to 6
- receiver_green: bfloat16 [4, 65536, 2, 256], P('freq', ('parts', 'slab')), parts along dimension 1, may hold values from -0.03125 to 0.03125
- observed: float32 [4, 32, 2, 128, 128], P('freq', ('parts', 'slab')), parts along dimension 1, may hold values from -6 to 6
- source_table: int32 [16, 2], P(('parts', 'slab')), parts along dimension 0, may hold values from 0 to 3, as said below
- receiver_table: int32 [16, 2], P(('parts', 'slab')), parts along dimension 0, may hold values from 0 to 3, as said below
Outputs:
- gradient: float32 [65536], P(('parts', 'slab', 'freq')), parts along dimension 0
- residual: float32 [4, 32, 2, 128, 128], P('freq', ('parts', 'slab')), parts along dimension 1
The draws below stay inside these ranges and needn't reach their ends.
There are 2 independent parts, one for each index of `parts`. The reference program is written for one: setup_inputs(seed, part) draws one part's arguments, and reference() takes and returns one part's arrays. A program takes and returns all parts, laid end to end along the dimension named above; each array names one. Nothing has to cross between parts.
Inputs may be any that keep to these rules, and one draw needn't show every extreme that they name: `source_table`: each row lists 2 different source blocks. `receiver_table`: each row lists 2 different receiver blocks.
All inputs are finite; a program needn't handle non-finite values.
Results may differ from the reference program's by a relative error of at most 0.0016.
Values may be sent and summed in bfloat16 or wider, within the bound.
A program may use at most 128 MiB of HBM per device.

```python
import jax
import jax.numpy as jnp
from jax import lax

BLK = 128
FREQS = 4
SB = 4
RB = 4
KS = 2
KR = 2
M_DEV = 4096
SLABS = 8
M = 32768
PANELS = 16


def station_rows(key, row_count, block_count, take_count):
    subkeys = jax.random.split(key, row_count)
    shuffled = jax.vmap(lambda one_key: jax.random.permutation(one_key, block_count))(subkeys)[:, :take_count]
    anchored = (block_count - 1 + jnp.arange(take_count)) % block_count
    leading = jnp.arange(row_count)[:, None] == 0
    return jnp.where(leading, anchored[None, :], shuffled).astype(jnp.int32)


def draw_source_table(key, part):
    return station_rows(jax.random.fold_in(key, 11), SLABS, SB, KS)


def draw_receiver_table(key, part):
    return station_rows(jax.random.fold_in(key, 23), SLABS, RB, KR)


def steps_of(stream_key, shape, cuts, smallest, largest):
    gain, own = 1.0, jax.random.fold_in(stream_key, 6)
    for axis_at, shards_of in cuts:
        draws = jnp.exp(jax.random.uniform(jax.random.fold_in(own, axis_at), (shards_of,), jnp.float32, smallest / len(cuts), largest / len(cuts)))
        gain = gain * jnp.repeat(draws, shape[axis_at] // shards_of).reshape([-1 if axis == axis_at else 1 for axis in range(len(shape))])
    return gain


def scatter_about(rng, shape, deviation, reach, cuts=(), kind=jnp.bfloat16):
    result = deviation * jax.random.normal(rng, shape, jnp.float32)
    if cuts:
        result = result * steps_of(rng, shape, cuts, -0.22, 0.18)
    return jnp.clip(result, -reach, reach).astype(kind)


def setup_inputs(seed: int = 0, part: int = 0) -> dict:
    key_of = jax.random.split(jax.random.key(seed), 7)
    own_keys = jax.random.split(jax.random.fold_in(key_of[6], part), 7)
    reflectivity = scatter_about(own_keys[0], (M,), 1.0, 6.0, ((0, 8),), jnp.float32)
    source_green = scatter_about(own_keys[1], (FREQS, M, 2, KS * BLK), 1.0, 6.0, ((0, 2), (1, 8)))
    receiver_green = scatter_about(own_keys[2], (FREQS, M, 2, KR * BLK), (8 * M_DEV) ** -0.5, 0.03125, ((0, 2), (1, 8)))
    observed = scatter_about(own_keys[3], (FREQS, PANELS, 2, BLK, BLK), 1.0, 6.0, ((0, 2), (1, 8)), jnp.float32)
    source_table = draw_source_table(jax.random.fold_in(jax.random.fold_in(key_of[6], part), 71), part)
    receiver_table = draw_receiver_table(jax.random.fold_in(jax.random.fold_in(key_of[6], part), 71), part)
    return {"reflectivity": reflectivity, "source_green": source_green, "receiver_green": receiver_green, "observed": observed, "source_table": source_table, "receiver_table": receiver_table}


def panel_ids_of(src_row, rec_row):
    return (src_row[:, None] * RB + rec_row[None, :]).reshape(-1).astype(jnp.int32)


def forward_panels(scaled_slab, rec_slab):
    products = jnp.einsum('fmas,fmbr->fasbr', scaled_slab.astype(jnp.float32), rec_slab.astype(jnp.float32))
    real_part = products[:, 0, :, 0, :] - products[:, 1, :, 1, :]
    imag_part = products[:, 0, :, 1, :] + products[:, 1, :, 0, :]
    stacked = jnp.stack([real_part, imag_part], axis=1)
    stacked = stacked.reshape(FREQS, 2, KS, BLK, KR, BLK).transpose(0, 2, 4, 1, 3, 5)
    return stacked.reshape(FREQS, KS * KR, 2, BLK, BLK)


def reference(reflectivity, source_green, receiver_green, observed, source_table, receiver_table):
    scaled = (source_green * reflectivity[None, :, None, None]).astype(jnp.bfloat16)
    slab_ids = jnp.arange(SLABS, dtype=jnp.int32)

    def add_slab(predicted, slab_id):
        first_point = (slab_id * M_DEV).astype(jnp.int32)
        scaled_slab = lax.dynamic_slice_in_dim(scaled, first_point, M_DEV, 1)
        rec_slab = lax.dynamic_slice_in_dim(receiver_green, first_point, M_DEV, 1)
        partial_value = forward_panels(scaled_slab, rec_slab)
        panel_ids = panel_ids_of(source_table[slab_id], receiver_table[slab_id])
        return predicted.at[:, panel_ids].add(partial_value), None

    start_pred = jnp.zeros((FREQS, PANELS, 2, BLK, BLK), jnp.float32)
    predicted, unused = lax.scan(add_slab, start_pred, slab_ids)
    residual = predicted - observed
    rounded = residual.astype(jnp.bfloat16)

    def slab_gradient(slab_id):
        first_point = (slab_id * M_DEV).astype(jnp.int32)
        src_slab = lax.dynamic_slice_in_dim(source_green, first_point, M_DEV, 1).astype(jnp.float32)
        rec_slab = lax.dynamic_slice_in_dim(receiver_green, first_point, M_DEV, 1).astype(jnp.float32)
        panel_ids = panel_ids_of(source_table[slab_id], receiver_table[slab_id])
        local_res = rounded[:, panel_ids].astype(jnp.float32)
        local_res = local_res.reshape(FREQS, KS, KR, 2, BLK, BLK).transpose(0, 1, 4, 3, 2, 5)
        local_res = local_res.reshape(FREQS, KS * BLK, 2, KR * BLK)
        products = jnp.einsum('fmas,fsbr->fmabr', src_slab, local_res)
        adj_real = products[:, :, 0, 0] + products[:, :, 1, 1]
        adj_imag = products[:, :, 0, 1] - products[:, :, 1, 0]
        slab_grad = rec_slab[:, :, 0] * adj_real + rec_slab[:, :, 1] * adj_imag
        return jnp.sum(slab_grad, axis=(0, 2))

    gradient = lax.map(slab_gradient, slab_ids).reshape(-1)
    return gradient, residual
```

```python
import functools

import jax
import jax.numpy as jnp
from jax import lax
from jax.experimental import pallas as pl
from jax.experimental.pallas import tpu as pltpu
from jax.sharding import PartitionSpec as P

RB = 4
TILE = 1024
SIDE = 2
GRID = (4, 2)
MESH = pl.DeviceIdType.MESH
F32 = jnp.float32
BF16 = jnp.bfloat16
I16 = jnp.int16
STRIP = 16
LEVELS = 256.0
REACH = 32600.0
VMEM_BYTES = 56 * 2**20
CUTS = 1


def encode(values, out):
    rows = values[0].shape[0]
    lanes = values[0].shape[1]
    line = lax.broadcasted_iota(jnp.int32, (STRIP, lanes), 0)
    peak = jnp.zeros((STRIP, lanes), F32)
    for at, value in enumerate(values):
        peak = jnp.where(line == at, jnp.max(jnp.abs(value), axis=0, keepdims=True), peak)
    level = jnp.ceil(jnp.log(jnp.maximum(peak, 1e-30)) * LEVELS) + 1.0
    gain = REACH * jnp.exp(level * (-1.0 / LEVELS))
    step = rows // STRIP
    out[len(values) * step] = level.astype(I16)
    for at, value in enumerate(values):
        code = jnp.round(value * gain[at : at + 1, :]).astype(I16)
        out[at * step : (at + 1) * step] = code.reshape(step, STRIP, lanes)


def decode_gains(src, gains, count, rows):
    level = src[count * (rows // STRIP)].astype(F32)
    gain = jnp.exp(level * (1.0 / LEVELS)) * (1.0 / REACH)
    for at in range(count):
        gains[at] = jnp.broadcast_to(gain[at : at + 1, :], gains.shape[1:])
    if count < gains.shape[0]:
        gains[count] = jnp.zeros(gains.shape[1:], F32)


def decode(src, gains, block, gain, rows):
    step = rows // STRIP
    codes = jnp.concatenate([src[block * step + at].astype(F32) for at in range(step)], axis=0)
    return codes * gains[gain][:1, :]


def grid_kernel(cuts, plan, st_ref, rt_ref, refl_ref, g_hbm, r_hbm, obs_ref, grad_ref, res_ref,
                raw, g32, r32, gd, rd, scaled, acc, part, adj, total, summed, other,
                tab_send, tab_recv, tab, obs_other, res_send, gains,
                cross_send, cross_recv, near_send, near_recv, far_recv, mid_send, mid_recv, end_send, end_recv,
                gath, last_send, last_recv,
                raw_sem, tab_ss, tab_rs, tab_local, obs_ss, obs_rs, res_ss, res_rs, cross_ss, cross_rs,
                near_ss, near_rs, far_ss, far_rs, mid_ss, mid_rs, end_ss, end_rs, ag_ss, ag_rs,
                last_ss, last_rs, ex_send, ex_recv):
    per = obs_ref.shape[1]
    lanes = obs_ref.shape[3]
    freqs, points, wide = gd.shape
    half = wide // 2
    tiles = points // TILE
    groups = TILE // lanes
    pairs = SIDE * SIDE
    tall = lanes // 2
    rows = tall // cuts
    span = pairs * rows
    me = lax.axis_index("slab")
    mine_f = lax.axis_index("freq")
    z = me // 2
    y = me % 2
    at_end = jnp.logical_or(z == 0, z == GRID[0] - 1)
    in_mid = jnp.logical_not(at_end)
    beside = z * 2 + 1 - y
    mid_z = 1 + z // 3
    end_z = 3 * (z - 1)
    across_z = 3 - z
    to_mid = mid_z * 2 + y
    to_end = end_z * 2 + y
    to_across = across_z * 2 + y
    mid_diag = mid_z * 2 + 1 - y
    end_diag = end_z * 2 + 1 - y

    def slab_id(index):
        return {"device_id": {"slab": index}, "device_id_type": MESH}

    chunks = [(f, c, q) for f in range(freqs) for c in range(2) for q in range(cuts)]

    barrier = pltpu.get_barrier_semaphore()
    pl.semaphore_signal(barrier, inc=1, **slab_id(beside))
    pl.semaphore_signal(barrier, inc=1, device_id={"freq": 1 - mine_f}, device_id_type=MESH)

    @pl.when(at_end)
    def _():
        pl.semaphore_signal(barrier, inc=1, **slab_id(to_mid))
        pl.semaphore_signal(barrier, inc=1, **slab_id(mid_diag))

    @pl.when(in_mid)
    def _():
        pl.semaphore_signal(barrier, inc=1, **slab_id(to_end))
        pl.semaphore_signal(barrier, inc=1, **slab_id(end_diag))
        pl.semaphore_signal(barrier, inc=1, **slab_id(to_across))

    def fetches(q, slot):
        return (
            pltpu.make_async_copy(g_hbm.at[q], raw.at[slot, 0], raw_sem.at[slot, 0]),
            pltpu.make_async_copy(r_hbm.at[q], raw.at[slot, 1], raw_sem.at[slot, 1]),
        )

    for q in range(2):
        for copy in fetches(q, q):
            copy.start()

    lane = lax.broadcasted_iota(jnp.int32, tab_send.shape, 1)
    line = jnp.zeros(tab_send.shape, jnp.int32)
    for at, value in enumerate((st_ref[0, 0], st_ref[0, 1], rt_ref[0, 0], rt_ref[0, 1])):
        line = jnp.where(lane == at, value, line)
    tab_send[...] = line

    def forward_tile(f, t):
        q = f * tiles + t
        slot = q % 2
        for copy in fetches(q, slot):
            copy.wait()
        g32[...] = raw[slot, 0].astype(F32)
        r32[...] = raw[slot, 1].astype(F32)

        @pl.when(q + 2 < freqs * tiles)
        def _():
            for copy in fetches(q + 2, slot):
                copy.start()

        refl = refl_ref[pl.ds(pl.multiple_of(t * groups, groups), groups), :]
        weight = jnp.concatenate(
            [jnp.broadcast_to(refl[b : b + 1, :], (lanes, lanes)).T for b in range(groups)], axis=0
        )
        here = pl.ds(pl.multiple_of(t * TILE, TILE), TILE)
        for block in range(SIDE):
            for comp in range(2):
                lines = pl.ds(block * 2 + comp, TILE, stride=2 * SIDE)
                cols = slice(comp * half + block * lanes, comp * half + (block + 1) * lanes)
                green = g32[lines, :]
                gd[f, here, cols] = green.astype(BF16)
                scaled[:, cols] = (green * weight).astype(BF16)
                rd[f, here, cols] = r32[lines, :].astype(BF16)
        prod = lax.dot_general(
            scaled[...], rd[f, here, :], (((0,), (0,)), ((), ())), preferred_element_type=F32
        )
        acc[...] += prod

    def forward(f, start, stop):
        def body(t, carry):
            forward_tile(f, t)
            return carry

        lax.fori_loop(start, stop, body, 0)

    def squares(i, j):
        s_re = slice(i * lanes, (i + 1) * lanes)
        s_im = slice(half + i * lanes, half + (i + 1) * lanes)
        r_re = slice(j * lanes, (j + 1) * lanes)
        r_im = slice(half + j * lanes, half + (j + 1) * lanes)
        return s_re, s_im, r_re, r_im

    def finish_part(f):
        for k in range(pairs):
            s_re, s_im, r_re, r_im = squares(k // SIDE, k % SIDE)
            part[f, k, 0] = acc[s_re, r_re] - acc[s_im, r_im]
            part[f, k, 1] = acc[s_re, r_im] + acc[s_im, r_re]
        part[f, pairs] = jnp.zeros((2, lanes, lanes), F32)

    own_table = (st_ref[0, 0], st_ref[0, 1], rt_ref[0, 0], rt_ref[0, 1])

    def table_of(slot):
        return tuple(tab[slot, 0, at] for at in range(4))

    def held_at(table, sb, rb):
        i = jnp.where(table[0] == sb, 0, jnp.where(table[1] == sb, SIDE, 2 * pairs))
        j = jnp.where(table[2] == rb, 0, jnp.where(table[3] == rb, 1, 2 * pairs))
        return jnp.minimum(i + j, pairs)

    def mine_rows(q):
        return pl.ds(pl.multiple_of(y * tall + q * rows, rows), rows)

    def their_rows(q):
        return pl.ds(pl.multiple_of((1 - y) * tall + q * rows, rows), rows)

    def remote(src, dst, send, recv, target):
        return pltpu.make_async_remote_copy(
            src_ref=src, dst_ref=dst, send_sem=send, recv_sem=recv, **slab_id(target)
        )

    def tab_copy(slot, target):
        return remote(tab_send, tab_recv.at[slot], tab_ss.at[slot], tab_rs.at[slot], target)

    def obs_copy():
        return remote(
            obs_ref.at[:, :, :, pl.ds(pl.multiple_of((1 - y) * tall, tall), tall), :],
            obs_other, obs_ss, obs_rs, beside,
        )

    def cross_copy(k):
        return remote(cross_send.at[k], cross_recv[k], cross_ss.at[k], cross_rs.at[k], beside)

    def near_copy(k):
        return remote(near_send.at[k], near_recv[k], near_ss.at[k], near_rs.at[k], to_mid)

    def far_copy(k):
        return remote(cross_recv[k], far_recv[k], far_ss.at[k], far_rs.at[k], to_mid)

    def mid_copy(k):
        return remote(mid_send.at[k], mid_recv.at[k], mid_ss.at[k], mid_rs.at[k], to_across)

    def end_copy(k):
        return remote(end_send.at[k], end_recv.at[k], end_ss.at[k], end_rs.at[k], to_end)

    def res_copy(k):
        f, c, q = chunks[k]
        return remote(res_send.at[k], res_ref.at[f, :, c, mine_rows(q), :], res_ss.at[k], res_rs.at[k], beside)

    def piece_copy(k, source, way, target):
        view = gath[k].at[pl.ds(pl.multiple_of(source * RB, RB), RB)]
        return remote(view, view, ag_ss.at[k, source, way], ag_rs.at[k, source], target)

    def last_copy(k):
        return remote(last_send.at[k], last_recv.at[k], last_ss.at[k], last_rs.at[k], beside)

    def greet():
        @pl.when(at_end)
        def _():
            pl.semaphore_wait(barrier, 4)
            tab_copy(1, to_mid).start()
            tab_copy(2, mid_diag).start()

        @pl.when(in_mid)
        def _():
            pl.semaphore_wait(barrier, 5)

        tab_copy(0, beside).start()
        obs_copy().start()

    def take_tables():
        tab_copy(0, beside).wait_recv()
        here = pltpu.make_async_copy(tab_recv.at[0], tab.at[0], tab_local.at[0])
        here.start()
        here.wait()

        @pl.when(in_mid)
        def _():
            for slot in (1, 2):
                tab_copy(slot, to_end).wait_recv()
                there = pltpu.make_async_copy(tab_recv.at[slot], tab.at[slot], tab_local.at[slot])
                there.start()
                there.wait()

    def share(k):
        f, c, q = chunks[k]
        encode([part[f, b, c, their_rows(q), :] for b in range(pairs)], cross_send.at[k])
        cross_copy(k).start()

        @pl.when(at_end)
        def _():
            encode([part[f, b, c, mine_rows(q), :] for b in range(pairs)], near_send.at[k])
            near_copy(k).start()

    def hand_on(k):
        cross_copy(k).wait_recv()
        far_copy(k).start()

    def term(src, k, slot, table, sb, rb):
        index = held_at(table, sb, rb)
        return decode(src, gains.at[k, slot], jnp.minimum(index, pairs - 1), index, rows)

    def own_term(k, sb, rb):
        f, c, q = chunks[k]
        return part[f, held_at(own_table, sb, rb), c, mine_rows(q), :]

    def mid_term(k, index):
        return decode(mid_recv.at[k], gains.at[k, 3], index, index, rows)

    def residuals(k, value_of):
        f, c, q = chunks[k]
        for at in range(per):
            rb = 2 * y + at
            value = value_of(rb) - obs_ref[f, at, c, mine_rows(q), :]
            res_ref[f, at, c, mine_rows(q), :] = value
            gath[k][z * RB + rb] = value.astype(BF16)
        for at in range(per):
            rb = 2 * (1 - y) + at
            value = value_of(rb) - obs_other[f, at, c, q * rows : (q + 1) * rows, :]
            res_send[k, at] = value
            gath[k][z * RB + rb] = value.astype(BF16)

    def merge(k):
        cross_copy(k).wait_recv()
        near_copy(k).wait_recv()
        far_copy(k).wait_recv()
        for slot, src in enumerate((cross_recv[k], near_recv[k], far_recv[k])):
            decode_gains(src, gains.at[k, slot], pairs, rows)
        tables = [table_of(slot) for slot in range(3)]
        values = []
        for s in range(2):
            sb = 2 * (2 - z) + s
            for rb in range(RB):
                value = own_term(k, sb, rb)
                for slot, src in enumerate((cross_recv[k], near_recv[k], far_recv[k])):
                    value = value + term(src, k, slot, tables[slot], sb, rb)
                values.append(value)
        encode(values, mid_send.at[k])
        mid_copy(k).start()

    def settle_mid(k):
        mid_copy(k).wait_recv()
        decode_gains(mid_recv.at[k], gains.at[k, 3], 2 * RB, rows)
        tables = [table_of(slot) for slot in range(3)]
        base = 2 * (z - 1)
        encode(
            [
                own_term(k, end_z, rb) + term(cross_recv[k], k, 0, tables[0], end_z, rb)
                + mid_term(k, (end_z - base) * RB + rb)
                for rb in range(RB)
            ],
            end_send.at[k],
        )
        end_copy(k).start()

        def value_of(rb):
            value = own_term(k, z, rb) + mid_term(k, (z - base) * RB + rb)
            for slot, src in enumerate((cross_recv[k], near_recv[k], far_recv[k])):
                value = value + term(src, k, slot, tables[slot], z, rb)
            return value

        residuals(k, value_of)
        piece_copy(k, z, 0, to_across).start()
        piece_copy(k, z, 1, to_end).start()
        res_copy(k).start()

    def settle_end(k):
        end_copy(k).wait_recv()
        decode_gains(cross_recv[k], gains.at[k, 0], pairs, rows)
        decode_gains(end_recv.at[k], gains.at[k, 3], RB, rows)
        table = table_of(0)

        def value_of(rb):
            return (
                own_term(k, z, rb) + term(cross_recv[k], k, 0, table, z, rb)
                + decode(end_recv.at[k], gains.at[k, 3], rb, rb, rows)
            )

        residuals(k, value_of)
        piece_copy(k, z, 0, to_mid).start()
        res_copy(k).start()

    def pass_across(k):
        piece_copy(k, end_z, 0, to_across).wait_recv()
        piece_copy(k, end_z, 0, to_across).start()

    def pass_first(k):
        piece_copy(k, across_z, 1, to_end).wait_recv()
        piece_copy(k, across_z, 1, to_end).start()

    def pass_second(k):
        piece_copy(k, 3 - end_z, 1, to_end).wait_recv()
        piece_copy(k, 3 - end_z, 1, to_end).start()

    def close_end(k):
        for source in (mid_z, 3 - mid_z, across_z):
            piece_copy(k, source, 0, to_mid).wait_recv()

    def give_last(k):
        table = table_of(0)
        for b in range(pairs):
            last_send[k, b] = gath[k][table[b // SIDE] * RB + table[2 + b % SIDE]]
        last_copy(k).start()

    def take_last(k):
        f, c, q = chunks[k]
        for b in range(pairs):
            i, j = b // SIDE, b % SIDE
            cols = slice(j * lanes, (j + 1) * lanes)
            ours = pl.ds(pl.multiple_of(i * lanes + y * tall + q * rows, rows), rows)
            adj[f, c, ours, cols] = gath[k][own_table[i] * RB + own_table[2 + j]]
        last_copy(k).wait_recv()
        for b in range(pairs):
            i, j = b // SIDE, b % SIDE
            cols = slice(j * lanes, (j + 1) * lanes)
            theirs = pl.ds(pl.multiple_of(i * lanes + (1 - y) * tall + q * rows, rows), rows)
            adj[f, c, theirs, cols] = last_recv[k, b]

    def adjoint_terms(f, c, t):
        here = pl.ds(pl.multiple_of(t * TILE, TILE), TILE)
        data = adj[f, c]
        by_re = jnp.dot(gd[f, here, :half], data, preferred_element_type=F32)
        by_im = jnp.dot(gd[f, here, half:], data, preferred_element_type=F32)
        rec_re = rd[f, here, :half].astype(F32)
        rec_im = rd[f, here, half:].astype(F32)
        if c == 0:
            terms = rec_re * by_re - rec_im * by_im
        else:
            terms = rec_re * by_im + rec_im * by_re
        result = terms[:, :lanes]
        for at in range(lanes, half, lanes):
            result = result + terms[:, at : at + lanes]
        return here, result

    def adjoint(f, c, start, stop):
        def body(t, carry):
            here, result = adjoint_terms(f, c, t)
            if f + c > 0:
                result = total[here, :] + result
            if f + c < 2:
                total[here, :] = result
                return carry
            sums = [
                jnp.sum(result[b * lanes : (b + 1) * lanes, :].T, axis=0, keepdims=True)
                for b in range(groups)
            ]
            summed[pl.ds(pl.multiple_of(t * groups, groups), groups), :] = jnp.concatenate(sums, 0)
            return carry

        lax.fori_loop(start, stop, body, 0)

    steps = {
        "share": share, "hand": hand_on, "merge": merge, "mid": settle_mid, "end": settle_end,
        "across": pass_across, "first": pass_first, "second": pass_second, "close": close_end,
        "give": give_last, "take": take_last,
    }

    def run(entry):
        kind = entry[0]
        if kind == "roles":
            for condition, todo in ((in_mid, entry[1]), (at_end, entry[2])):
                if todo:
                    @pl.when(condition)
                    def _():
                        for name, k in todo:
                            steps[name](k)
        elif kind == "greet":
            greet()
        elif kind == "tables":
            take_tables()
        elif kind == "forward":
            if entry[2] == 0:
                acc[...] = jnp.zeros_like(acc)
            forward(*entry[1:])
            if entry[3] == tiles:
                finish_part(entry[1])
        elif kind == "obs":
            obs_copy().wait_recv()
        elif kind == "adjoint":
            adjoint(*entry[1:])
        else:
            steps[kind](entry[1])

    for entry in plan(tiles, cuts):
        run(entry)

    own_rows = grad_ref.shape[0]
    swap = pltpu.make_async_remote_copy(
        src_ref=summed.at[pl.ds(pl.multiple_of((1 - mine_f) * own_rows, own_rows), own_rows)],
        dst_ref=other,
        send_sem=ex_send,
        recv_sem=ex_recv,
        device_id={"freq": 1 - mine_f},
        device_id_type=MESH,
    )
    swap.start()

    tab_copy(0, beside).wait_send()
    obs_copy().wait_send()
    for k in range(len(chunks)):
        cross_copy(k).wait_send()
        last_copy(k).wait_send()
        res_copy(k).wait()

    @pl.when(at_end)
    def _():
        tab_copy(1, to_mid).wait_send()
        tab_copy(2, mid_diag).wait_send()
        for k in range(len(chunks)):
            near_copy(k).wait_send()
            far_copy(k).wait_send()
            piece_copy(k, z, 0, to_mid).wait_send()

    @pl.when(in_mid)
    def _():
        for k in range(len(chunks)):
            mid_copy(k).wait_send()
            end_copy(k).wait_send()
            piece_copy(k, z, 0, to_across).wait_send()
            piece_copy(k, end_z, 0, to_across).wait_send()
            piece_copy(k, z, 1, to_end).wait_send()
            piece_copy(k, across_z, 1, to_end).wait_send()
            piece_copy(k, 3 - end_z, 1, to_end).wait_send()

    swap.wait()
    mine = summed[pl.ds(pl.multiple_of(mine_f * own_rows, own_rows), own_rows), :]
    grad_ref[...] = mine + other[...]


def grid_plan(tiles, cuts):
    part = [list(range(a * cuts, (a + 1) * cuts)) for a in range(4)]
    early, late = part[0] + part[1], part[2] + part[3]
    plan = [("forward", 0, 0, 1), ("greet",), ("forward", 0, 1, tiles)]
    plan += [("share", k) for k in early]
    plan += [("forward", 1, 0, tiles // 2), ("tables",), ("obs",)]
    plan += [("roles", [], [("hand", k) for k in early])]
    plan += [("forward", 1, tiles // 2, tiles)]
    plan += [("share", k) for k in late]
    n = 4 * cuts
    plan += [("roles", [("merge", k) for k in early], [("hand", k) for k in late])]
    for k in range(n):
        mids = [("mid", k)]
        if k + len(early) < n:
            mids.append(("merge", k + len(early)))
        if k >= 1:
            mids += [("first", k - 1), ("across", k - 1)]
        if k >= 2:
            mids += [("second", k - 2), ("give", k - 2)]
        ends = [("end", k)]
        if k >= 2:
            ends += [("close", k - 2), ("give", k - 2)]
        plan += [("roles", mids, ends)]
    plan += [("roles", [("first", n - 1), ("across", n - 1), ("second", n - 2), ("give", n - 2), ("second", n - 1), ("give", n - 1)],
              [("close", n - 2), ("give", n - 2), ("close", n - 1), ("give", n - 1)])]
    for a in range(4):
        plan += [("take", k) for k in part[a]]
        plan += [("adjoint", a // 2, a % 2, 0, tiles)]
    return plan


def ring_kernel(n, snake, st_ref, rt_ref, refl_ref, g_hbm, r_hbm, obs_ref, grad_ref, res_ref,
           raw, g32, r32, gd, rd, scaled, acc, part, first, held, gath_a, gath_b, gath_c, gath_d, adj, total, summed, other,
           raw_sem, rs_send, rs_recv, ag_send, ag_recv, ex_send, ex_recv):
    per = obs_ref.shape[1]
    lanes = obs_ref.shape[3]
    freqs, points, wide = gd.shape
    half = wide // 2
    tiles = points // TILE
    groups = TILE // lanes
    pairs = SIDE * SIDE
    gath = ((gath_a, gath_b), (gath_c, gath_d))
    me = lax.axis_index("slab")
    mine_f = lax.axis_index("freq")

    def index_of(pos):
        if not snake:
            return pos
        return 2 * pos + (pos // (n // 2)) * (2 * n - 1 - 4 * pos)

    place = me // 2 + (me % 2) * (n - 1 - 2 * (me // 2)) if snake else me
    ways = (1, -1)
    targets = tuple(index_of((place + way + n) % n) for way in ways)
    low = (n - 1) // 2
    high = n - 1 - low

    barrier = pltpu.get_barrier_semaphore()
    for target in targets:
        pl.semaphore_signal(barrier, inc=1, device_id={"slab": target}, device_id_type=MESH)
    pl.semaphore_signal(barrier, inc=1, device_id={"freq": 1 - mine_f}, device_id_type=MESH)

    def fetches(q, slot):
        return (
            pltpu.make_async_copy(g_hbm.at[q], raw.at[slot, 0], raw_sem.at[slot, 0]),
            pltpu.make_async_copy(r_hbm.at[q], raw.at[slot, 1], raw_sem.at[slot, 1]),
        )

    for q in range(2):
        for copy in fetches(q, q):
            copy.start()

    def forward_tile(f, t):
        q = f * tiles + t
        slot = q % 2
        for copy in fetches(q, slot):
            copy.wait()
        g32[...] = raw[slot, 0].astype(F32)
        r32[...] = raw[slot, 1].astype(F32)

        @pl.when(q + 2 < freqs * tiles)
        def _():
            for copy in fetches(q + 2, slot):
                copy.start()

        refl = refl_ref[pl.ds(pl.multiple_of(t * groups, groups), groups), :]
        weight = jnp.concatenate(
            [jnp.broadcast_to(refl[b : b + 1, :], (lanes, lanes)).T for b in range(groups)], axis=0
        )
        here = pl.ds(pl.multiple_of(t * TILE, TILE), TILE)
        for block in range(SIDE):
            for comp in range(2):
                rows = pl.ds(block * 2 + comp, TILE, stride=2 * SIDE)
                cols = slice(comp * half + block * lanes, comp * half + (block + 1) * lanes)
                green = g32[rows, :]
                gd[f, here, cols] = green.astype(BF16)
                scaled[:, cols] = (green * weight).astype(BF16)
                rd[f, here, cols] = r32[rows, :].astype(BF16)
        prod = lax.dot_general(
            scaled[...], rd[f, here, :], (((0,), (0,)), ((), ())), preferred_element_type=F32
        )
        acc[...] += prod

    def forward(f, start, stop):
        def body(t, carry):
            forward_tile(f, t)
            return carry

        lax.fori_loop(start, stop, body, 0)

    def squares(i, j):
        s_re = slice(i * lanes, (i + 1) * lanes)
        s_im = slice(half + i * lanes, half + (i + 1) * lanes)
        r_re = slice(j * lanes, (j + 1) * lanes)
        r_im = slice(half + j * lanes, half + (j + 1) * lanes)
        return s_re, s_im, r_re, r_im

    def finish_part(f):
        for k in range(pairs):
            s_re, s_im, r_re, r_im = squares(k // SIDE, k % SIDE)
            part[f, k, 0] = acc[s_re, r_re] - acc[s_im, r_im]
            part[f, k, 1] = acc[s_re, r_im] + acc[s_im, r_re]
        part[f, pairs] = jnp.zeros((2, lanes, lanes), F32)

    def hops(f, w):
        return high if f == w else low

    lanes_of = [(c, w) for c in range(2) for w in range(2)]

    def held_at(panel):
        sb = panel // RB
        rb = panel % RB
        i = jnp.where(st_ref[0, 0] == sb, 0, jnp.where(st_ref[0, 1] == sb, SIDE, 2 * pairs))
        j = jnp.where(rt_ref[0, 0] == rb, 0, jnp.where(rt_ref[0, 1] == rb, 1, 2 * pairs))
        return jnp.minimum(i + j, pairs)

    def own(f, c, w, away):
        owner = index_of((place + ways[w] * away + n) % n)
        return [part[f, held_at(owner * per + k), c] for k in range(per)]

    def rs_copy(f, c, w, src, step):
        return pltpu.make_async_remote_copy(
            src_ref=src,
            dst_ref=held.at[f, c, w, step],
            send_sem=rs_send.at[f, c, w, step],
            recv_sem=rs_recv.at[f, c, w, step],
            device_id={"slab": targets[w]},
            device_id_type=MESH,
        )

    def ag_copy(f, c, w, step, away):
        owner = index_of((place - ways[w] * away + n) % n)
        view = gath[f][c].at[pl.ds(owner * per, per)]
        return pltpu.make_async_remote_copy(
            src_ref=view,
            dst_ref=view,
            send_sem=ag_send.at[f, c, w, step],
            recv_sem=ag_recv.at[f, c, w, step],
            device_id={"slab": targets[w]},
            device_id_type=MESH,
        )

    def rs_start(f):
        for c, w in lanes_of:
            mine = own(f, c, w, hops(f, w))
            for k in range(per):
                first[f, c, w, k] = mine[k]
            rs_copy(f, c, w, first.at[f, c, w], 0).start()

    def rs_pass(f, step, only=None):
        for c, w in lanes_of:
            if only is not None and w != only:
                continue
            rs_copy(f, c, w, held.at[f, c, w, step], step).wait_recv()
            mine = own(f, c, w, hops(f, w) - step - 1)
            for k in range(per):
                held[f, c, w, step, k] = held[f, c, w, step, k] + mine[k]
            rs_copy(f, c, w, held.at[f, c, w, step], step + 1).start()

    def ag_pass(f, step, only=None):
        for c, w in lanes_of:
            if only is not None and w != only:
                continue
            ag_copy(f, c, w, step, step + 1).wait_recv()
            ag_copy(f, c, w, step + 1, step + 1).start()

    def rs_longer(f):
        if high > low:
            rs_pass(f, high - 2, f)

    def ag_longer(f):
        if high > low:
            ag_pass(f, high - 2, f)

    def rs_finish(f):
        for c in range(2):
            for w in range(2):
                last = hops(f, w) - 1
                rs_copy(f, c, w, held.at[f, c, w, last], last).wait_recv()
            mine = own(f, c, 0, 0)
            for k in range(per):
                value = (
                    held[f, c, 0, hops(f, 0) - 1, k] + held[f, c, 1, hops(f, 1) - 1, k] + mine[k]
                ) - obs_ref[f, k, c]
                res_ref[f, k, c] = value
                gath[f][c][me * per + k] = value.astype(BF16)
            for w in range(2):
                ag_copy(f, c, w, 0, 0).start()

    def ag_finish(f, c):
        for w in range(2):
            last = hops(f, w) - 1
            ag_copy(f, c, w, last, last + 1).wait_recv()
        for k in range(pairs):
            i, j = k // SIDE, k % SIDE
            panel = st_ref[0, i] * RB + rt_ref[0, j]
            s_re, s_im, r_re, r_im = squares(i, j)
            adj[f, c, s_re, r_re] = gath[f][c][panel]

    def adjoint_terms(f, c, t):
        here = pl.ds(pl.multiple_of(t * TILE, TILE), TILE)
        data = adj[f, c]
        by_re = jnp.dot(gd[f, here, :half], data, preferred_element_type=F32)
        by_im = jnp.dot(gd[f, here, half:], data, preferred_element_type=F32)
        rec_re = rd[f, here, :half].astype(F32)
        rec_im = rd[f, here, half:].astype(F32)
        if c == 0:
            terms = rec_re * by_re - rec_im * by_im
        else:
            terms = rec_re * by_im + rec_im * by_re
        result = terms[:, :lanes]
        for at in range(lanes, half, lanes):
            result = result + terms[:, at : at + lanes]
        return here, result

    def adjoint(f, c):
        def body(t, carry):
            here, result = adjoint_terms(f, c, t)
            if f + c > 0:
                result = total[here, :] + result
            if f + c < 2:
                total[here, :] = result
                return carry
            rows = [
                jnp.sum(result[b * lanes : (b + 1) * lanes, :].T, axis=0, keepdims=True)
                for b in range(groups)
            ]
            summed[pl.ds(pl.multiple_of(t * groups, groups), groups), :] = jnp.concatenate(rows, 0)
            return carry

        lax.fori_loop(0, tiles, body, 0)

    acc[...] = jnp.zeros_like(acc)
    forward(0, 0, tiles)
    finish_part(0)
    pl.semaphore_wait(barrier, 3)
    rs_start(0)
    acc[...] = jnp.zeros_like(acc)
    forward(1, 0, tiles // 2)
    rs_pass(0, 0)
    forward(1, tiles // 2, tiles)
    finish_part(1)
    rs_start(1)

    def rs_both(step, carry):
        rs_pass(0, step)
        rs_pass(1, step - 1)
        return carry

    lax.fori_loop(1, low - 1, rs_both, 0)
    rs_longer(0)
    rs_pass(1, low - 2)
    rs_finish(0)
    rs_longer(1)
    ag_pass(0, 0)
    rs_finish(1)

    def ag_both(step, carry):
        ag_pass(0, step)
        ag_pass(1, step - 1)
        return carry

    lax.fori_loop(1, low - 1, ag_both, 0)
    ag_longer(0)
    ag_pass(1, low - 2)
    ag_finish(0, 0)
    adjoint(0, 0)
    ag_longer(1)
    ag_finish(0, 1)
    adjoint(0, 1)
    ag_finish(1, 0)
    adjoint(1, 0)
    ag_finish(1, 1)
    adjoint(1, 1)

    own_rows = grad_ref.shape[0]
    swap = pltpu.make_async_remote_copy(
        src_ref=summed.at[pl.ds(pl.multiple_of((1 - mine_f) * own_rows, own_rows), own_rows)],
        dst_ref=other,
        send_sem=ex_send,
        recv_sem=ex_recv,
        device_id={"freq": 1 - mine_f},
        device_id_type=MESH,
    )
    swap.start()

    def drain(step, carry):
        for f in range(2):
            for c, w in lanes_of:
                rs_copy(f, c, w, first.at[f, c, w], step).wait_send()
                ag_copy(f, c, w, step, step).wait_send()
        return carry

    lax.fori_loop(0, low, drain, 0)
    if high > low:
        for f in range(2):
            for c in range(2):
                rs_copy(f, c, f, first.at[f, c, f], high - 1).wait_send()
                ag_copy(f, c, f, high - 1, high - 1).wait_send()
    swap.wait()
    mine = summed[pl.ds(pl.multiple_of(mine_f * own_rows, own_rows), own_rows), :]
    grad_ref[...] = mine + other[...]


def interleaved_tiles(green, lanes):
    freqs, points, comps, width = green.shape
    view = green.reshape(freqs, points, comps, width // lanes, lanes).transpose(0, 1, 3, 2, 4)
    tiles = freqs * points // TILE
    return view.reshape(tiles, TILE * comps * width // lanes, lanes)


def grid_on_device(reflectivity, source_green, receiver_green, observed, source_table, receiver_table):
    freqs, points, comps, width = source_green.shape
    per = observed.shape[1]
    lanes = observed.shape[3]
    pairs = SIDE * SIDE
    panels = RB * GRID[0]
    wide = comps * width
    tall = TILE * wide // lanes
    lines = points // lanes
    cuts = CUTS
    rows = lanes // 2 // cuts
    count = 2 * freqs * cuts
    four = pairs * rows // STRIP + 1
    eight = 2 * pairs * rows // STRIP + 1
    vmem = pl.BlockSpec(memory_space=pltpu.VMEM)
    smem = pl.BlockSpec(memory_space=pltpu.SMEM)
    hbm = pl.BlockSpec(memory_space=pl.ANY)
    sem = pltpu.SemaphoreType.DMA
    gradient, residual = pl.pallas_call(
        functools.partial(grid_kernel, cuts, grid_plan),
        in_specs=[smem, smem, vmem, hbm, hbm, vmem],
        out_specs=[vmem, vmem],
        out_shape=[
            jax.ShapeDtypeStruct((lines // 2, lanes), F32),
            jax.ShapeDtypeStruct(observed.shape, F32),
        ],
        scratch_shapes=[
            pltpu.VMEM((2, 2, tall, lanes), BF16),
            pltpu.VMEM((tall, lanes), F32),
            pltpu.VMEM((tall, lanes), F32),
            pltpu.VMEM((freqs, points, wide), BF16),
            pltpu.VMEM((freqs, points, wide), BF16),
            pltpu.VMEM((TILE, wide), BF16),
            pltpu.VMEM((wide, wide), F32),
            pltpu.VMEM((freqs, pairs + 1, 2, lanes, lanes), F32),
            pltpu.VMEM((freqs, 2, width, width), BF16),
            pltpu.VMEM((points, lanes), F32),
            pltpu.VMEM((lines, lanes), F32),
            pltpu.VMEM((lines // 2, lanes), F32),
            pltpu.VMEM((8, 128), jnp.int32),
            pltpu.VMEM((3, 8, 128), jnp.int32),
            pltpu.SMEM((3, 8, 128), jnp.int32),
            pltpu.VMEM((freqs, per, 2, lanes // 2, lanes), F32),
            pltpu.VMEM((count, per, rows, lanes), F32),
            pltpu.VMEM((count, 4, 2 * pairs, 8, lanes), F32),
            pltpu.VMEM((count, four, STRIP, lanes), I16),
            [pltpu.VMEM((four, STRIP, lanes), I16)] * count,
            pltpu.VMEM((count, four, STRIP, lanes), I16),
            [pltpu.VMEM((four, STRIP, lanes), I16)] * count,
            [pltpu.VMEM((four, STRIP, lanes), I16)] * count,
            pltpu.VMEM((count, eight, STRIP, lanes), I16),
            pltpu.VMEM((count, eight, STRIP, lanes), I16),
            pltpu.VMEM((count, four, STRIP, lanes), I16),
            pltpu.VMEM((count, four, STRIP, lanes), I16),
            [pltpu.VMEM((panels, rows, lanes), BF16)] * count,
            pltpu.VMEM((count, pairs, rows, lanes), BF16),
            pltpu.VMEM((count, pairs, rows, lanes), BF16),
            sem((2, 2)),
            sem((3,)), sem((3,)), sem((3,)),
            sem, sem,
            sem((count,)), sem((count,)),
            sem((count,)), sem((count,)),
            sem((count,)), sem((count,)),
            sem((count,)), sem((count,)),
            sem((count,)), sem((count,)),
            sem((count,)), sem((count,)),
            sem((count, GRID[0], 2)), sem((count, GRID[0])),
            sem((count,)), sem((count,)),
            sem, sem,
        ],
        compiler_params=pltpu.CompilerParams(
            collective_id=0, has_side_effects=True, vmem_limit_bytes=VMEM_BYTES
        ),
        name="migration",
    )(
        source_table,
        receiver_table,
        reflectivity.reshape(lines, lanes),
        interleaved_tiles(source_green, lanes),
        interleaved_tiles(receiver_green, lanes),
        observed,
    )
    return gradient.reshape(points // 2), residual


def ring_on_device(reflectivity, source_green, receiver_green, observed, source_table, receiver_table):
    freqs, points, comps, width = source_green.shape
    per = observed.shape[1]
    lanes = observed.shape[3]
    n = lax.axis_size("slab")
    pairs = SIDE * SIDE
    wide = comps * width
    tall = TILE * wide // lanes
    rows = points // lanes
    vmem = pl.BlockSpec(memory_space=pltpu.VMEM)
    smem = pl.BlockSpec(memory_space=pltpu.SMEM)
    hbm = pl.BlockSpec(memory_space=pl.ANY)
    hop_sems = pltpu.SemaphoreType.DMA((freqs, 2, 2, n // 2))
    gradient, residual = pl.pallas_call(
        functools.partial(ring_kernel, n, n == 8),
        in_specs=[smem, smem, vmem, hbm, hbm, vmem],
        out_specs=[vmem, vmem],
        out_shape=[
            jax.ShapeDtypeStruct((rows // 2, lanes), F32),
            jax.ShapeDtypeStruct(observed.shape, F32),
        ],
        scratch_shapes=[
            pltpu.VMEM((2, 2, tall, lanes), BF16),
            pltpu.VMEM((tall, lanes), F32),
            pltpu.VMEM((tall, lanes), F32),
            pltpu.VMEM((freqs, points, wide), BF16),
            pltpu.VMEM((freqs, points, wide), BF16),
            pltpu.VMEM((TILE, wide), BF16),
            pltpu.VMEM((wide, wide), F32),
            pltpu.VMEM((freqs, pairs + 1, 2, lanes, lanes), F32),
            pltpu.VMEM((freqs, 2, 2, per, lanes, lanes), F32),
            pltpu.VMEM((freqs, 2, 2, n // 2, per, lanes, lanes), F32),
            pltpu.VMEM((n * per, lanes, lanes), BF16),
            pltpu.VMEM((n * per, lanes, lanes), BF16),
            pltpu.VMEM((n * per, lanes, lanes), BF16),
            pltpu.VMEM((n * per, lanes, lanes), BF16),
            pltpu.VMEM((freqs, 2, width, width), BF16),
            pltpu.VMEM((points, lanes), F32),
            pltpu.VMEM((rows, lanes), F32),
            pltpu.VMEM((rows // 2, lanes), F32),
            pltpu.SemaphoreType.DMA((2, 2)),
            hop_sems,
            hop_sems,
            hop_sems,
            hop_sems,
            pltpu.SemaphoreType.DMA,
            pltpu.SemaphoreType.DMA,
        ],
        compiler_params=pltpu.CompilerParams(collective_id=0, has_side_effects=True, vmem_limit_bytes=VMEM_BYTES),
        name="migration",
    )(
        source_table,
        receiver_table,
        reflectivity.reshape(rows, lanes),
        interleaved_tiles(source_green, lanes),
        interleaved_tiles(receiver_green, lanes),
        observed,
    )
    return gradient.reshape(points // 2), residual


def solution(mesh):
    on_device = grid_on_device if mesh.shape["slab"] == GRID[0] * GRID[1] else ring_on_device
    return jax.shard_map(
        on_device,
        mesh=mesh,
        in_specs=(
            P(("parts", "slab")),
            P("freq", ("parts", "slab"), None, None),
            P("freq", ("parts", "slab"), None, None),
            P("freq", ("parts", "slab"), None, None, None),
            P(("parts", "slab"), None),
            P(("parts", "slab"), None),
        ),
        out_specs=(P(("parts", "slab", "freq")), P("freq", ("parts", "slab"), None, None, None)),
        check_vma=False,
    )
```

```python
import functools

import jax
import jax.numpy as jnp
from jax import lax
from jax.experimental import pallas as pl
from jax.experimental.pallas import tpu as pltpu
from jax.sharding import PartitionSpec as P

RB = 4
TILE = 1024
SIDE = 2
MESH = pl.DeviceIdType.MESH
F32 = jnp.float32
BF16 = jnp.bfloat16
I16 = jnp.int16
STRIP = 16
SLICES = 8
LEVELS = 256.0
REACH = 32600.0
VMEM_BYTES = 56 * 2**20


def encode_slices(values, out):
    count = out.shape[0]
    lanes = values[0].shape[1]
    line = lax.broadcasted_iota(jnp.int32, (STRIP, lanes), 0)
    peak = jnp.zeros((STRIP, lanes), F32)
    for at, value in enumerate(values):
        peak = jnp.where(line == at, jnp.max(jnp.abs(value), axis=0, keepdims=True), peak)
    level = jnp.ceil(jnp.log(jnp.maximum(peak, 1e-30)) * LEVELS) + 1.0
    gain = REACH * jnp.exp(level * (-1.0 / LEVELS))
    level = level.astype(I16)
    for at in range(count):
        out[at, 0] = level
    for at, value in enumerate(values):
        code = jnp.round(value * gain[at : at + 1, :]).astype(I16)
        out[:, 1 + at] = code.reshape(count, STRIP, lanes)


def gains_of(level):
    return jnp.exp(level.astype(F32) * (1.0 / LEVELS)) * (1.0 / REACH)


def grid_kernel(plan, st_ref, rt_ref, refl_ref, g_hbm, r_hbm, obs_ref, grad_ref, res_ref,
                raw, g32, r32, gd, rd, scaled, acc, part, adj, total, summed, other,
                tab_send, tab_recv, tab, obs_send, obs_recv, obs_all, sum_send, sum_recv, terms,
                res_all, rounded, use_send, ret_send, ret_recv,
                raw_sem, tab_ss, tab_rs, tab_local, obs_ss, obs_rs, sum_ss, sum_rs, use_ss, use_rs,
                ret_ss, ret_rs, ex_send, ex_recv):
    per = obs_ref.shape[1]
    lanes = obs_ref.shape[3]
    freqs, points, wide = gd.shape
    half = wide // 2
    tiles = points // TILE
    groups = TILE // lanes
    pairs = SIDE * SIDE
    n = lanes // STRIP
    panels = n * per
    me = lax.axis_index("slab")
    mine_f = lax.axis_index("freq")
    order = sorted(range(1, n), key=lambda d: abs(d - n // 2))

    def to(d):
        return lax.rem(me + d, n)

    def source(d):
        return lax.rem(me + n - d, n)

    def strip(at):
        return pl.ds(pl.multiple_of(at * STRIP, STRIP), STRIP)

    barrier = pltpu.get_barrier_semaphore()
    for d in order:
        pl.semaphore_signal(barrier, inc=1, device_id={"slab": to(d)}, device_id_type=MESH)
    pl.semaphore_signal(barrier, inc=1, device_id={"freq": 1 - mine_f}, device_id_type=MESH)

    def fetches(q, slot):
        return (
            pltpu.make_async_copy(g_hbm.at[q], raw.at[slot, 0], raw_sem.at[slot, 0]),
            pltpu.make_async_copy(r_hbm.at[q], raw.at[slot, 1], raw_sem.at[slot, 1]),
        )

    for q in range(2):
        for copy in fetches(q, q):
            copy.start()

    lane = lax.broadcasted_iota(jnp.int32, tab_send.shape, 1)
    line = jnp.zeros(tab_send.shape, jnp.int32)
    for at, value in enumerate((st_ref[0, 0], st_ref[0, 1], rt_ref[0, 0], rt_ref[0, 1])):
        line = jnp.where(lane == at, value, line)
    tab_send[...] = line
    tab_recv[me] = line
    terms[:, pairs] = jnp.zeros((n, STRIP, lanes), F32)

    def forward_tile(f, t):
        q = f * tiles + t
        slot = q % 2
        for copy in fetches(q, slot):
            copy.wait()
        g32[...] = raw[slot, 0].astype(F32)
        r32[...] = raw[slot, 1].astype(F32)

        @pl.when(q + 2 < freqs * tiles)
        def _():
            for copy in fetches(q + 2, slot):
                copy.start()

        refl = refl_ref[pl.ds(pl.multiple_of(t * groups, groups), groups), :]
        weight = jnp.concatenate(
            [jnp.broadcast_to(refl[b : b + 1, :], (lanes, lanes)).T for b in range(groups)], axis=0
        )
        here = pl.ds(pl.multiple_of(t * TILE, TILE), TILE)
        for block in range(SIDE):
            for comp in range(2):
                lines = pl.ds(block * 2 + comp, TILE, stride=2 * SIDE)
                cols = slice(comp * half + block * lanes, comp * half + (block + 1) * lanes)
                green = g32[lines, :]
                gd[f, here, cols] = green.astype(BF16)
                scaled[:, cols] = (green * weight).astype(BF16)
                rd[f, here, cols] = r32[lines, :].astype(BF16)
        prod = lax.dot_general(
            scaled[...], rd[f, here, :], (((0,), (0,)), ((), ())), preferred_element_type=F32
        )
        acc[...] += prod

    def forward(f, start, stop):
        def body(t, carry):
            forward_tile(f, t)
            return carry

        lax.fori_loop(start, stop, body, 0)

    def squares(i, j):
        s_re = slice(i * lanes, (i + 1) * lanes)
        s_im = slice(half + i * lanes, half + (i + 1) * lanes)
        r_re = slice(j * lanes, (j + 1) * lanes)
        r_im = slice(half + j * lanes, half + (j + 1) * lanes)
        return s_re, s_im, r_re, r_im

    def finish_part(f):
        for k in range(pairs):
            s_re, s_im, r_re, r_im = squares(k // SIDE, k % SIDE)
            part[f, k, 0] = acc[s_re, r_re] - acc[s_im, r_im]
            part[f, k, 1] = acc[s_re, r_im] + acc[s_im, r_re]

    def remote(src, dst, send, recv, d):
        return pltpu.make_async_remote_copy(
            src_ref=src, dst_ref=dst, send_sem=send, recv_sem=recv,
            device_id={"slab": to(d)}, device_id_type=MESH,
        )

    def tab_copy(d, at):
        return remote(tab_send, tab_recv.at[at], tab_ss.at[d], tab_rs.at[d], d)

    def obs_copy(d, at):
        return remote(obs_send.at[to(d)], obs_recv.at[at], obs_ss.at[d], obs_rs.at[d], d)

    def sum_copy(f, c, d, at):
        part_of = pl.ds(0, pairs + 1) if c == 0 else pl.ds(pairs + 1, pairs)
        return remote(
            sum_send.at[f, to(d), part_of], sum_recv.at[f, at, part_of],
            sum_ss.at[f, c, d], sum_rs.at[f, c, d], d,
        )

    def use_copy(f, c, d, at):
        return remote(
            use_send.at[f, c, to(d)], adj.at[f, c, :, strip(at), :],
            use_ss.at[f, c, d], use_rs.at[f, c, d], d,
        )

    def ret_copy(d, at):
        return remote(ret_send.at[to(d)], ret_recv.at[at], ret_ss.at[d], ret_rs.at[d], d)

    def greet():
        pl.semaphore_wait(barrier, n)
        for d in order:
            tab_copy(d, me).start()

    def give_obs():
        encode_slices(
            [obs_ref[f, k, c] for f in range(freqs) for c in range(2) for k in range(per)], obs_send
        )
        for d in order:
            obs_copy(d, me).start()

    def take_tables():
        for d in order:
            tab_copy(d, source(d)).wait_recv()
        copy = pltpu.make_async_copy(tab_recv, tab, tab_local)
        copy.start()
        copy.wait()

    def take_obs():
        for d in order:
            at = source(d)
            obs_copy(d, at).wait_recv()
            gains = gains_of(obs_recv[at, 0])
            block = 0
            for f in range(freqs):
                for c in range(2):
                    for k in range(per):
                        obs_all[f, c, at * per + k] = (
                            obs_recv[at, 1 + block].astype(F32) * gains[block : block + 1, :]
                        )
                        block += 1
        for f in range(freqs):
            for c in range(2):
                for k in range(per):
                    obs_all[f, c, me * per + k] = obs_ref[f, k, c, strip(me), :]

    def share(f):
        encode_slices([part[f, b, c] for c in range(2) for b in range(pairs)], sum_send.at[f])
        for c in range(2):
            for d in order:
                sum_copy(f, c, d, me).start()

    def tables():
        return [tuple(tab[s, 0, at] for at in range(4)) for s in range(n)]

    def reduce(f, c):
        for b in range(pairs):
            terms[me, b] = part[f, b, c, strip(me), :]
        for d in order:
            at = source(d)
            sum_copy(f, c, d, at).wait_recv()
            gains = gains_of(sum_recv[f, at, 0])
            for b in range(pairs):
                block = c * pairs + b
                terms[at, b] = sum_recv[f, at, 1 + block].astype(F32) * gains[block : block + 1, :]
        rows_of, cols_of = [], []
        for table in tables():
            rows_of.append([
                jnp.where(table[0] == sb, 0, jnp.where(table[1] == sb, SIDE, pairs))
                for sb in range(panels // RB)
            ])
            cols_of.append([
                jnp.where(table[2] == rb, 0, jnp.where(table[3] == rb, 1, pairs)) for rb in range(RB)
            ])
        for panel in range(panels):
            value = -obs_all[f, c, panel]
            for s in range(n):
                index = jnp.minimum(rows_of[s][panel // RB] + cols_of[s][panel % RB], pairs)
                value = value + terms[s, index]
            res_all[f, c, panel] = value
            rounded[panel] = value.astype(BF16)
        for at, table in enumerate(tables()):
            for b in range(pairs):
                use_send[f, c, at, b] = rounded[table[b // SIDE] * RB + table[2 + b % SIDE]]
        for d in order:
            use_copy(f, c, d, me).start()
        for b in range(pairs):
            adj[f, c, b, strip(me), :] = use_send[f, c, me, b]

    def give_back():
        line = lax.broadcasted_iota(jnp.int32, (STRIP, lanes), 0)
        for at in range(n):
            peak = jnp.zeros((STRIP, lanes), F32)
            blocks = [(f, c, k) for f in range(freqs) for c in range(2) for k in range(per)]
            for block, (f, c, k) in enumerate(blocks):
                value = res_all[f, c, at * per + k]
                peak = jnp.where(line == block, jnp.max(jnp.abs(value), axis=0, keepdims=True), peak)
            level = jnp.ceil(jnp.log(jnp.maximum(peak, 1e-30)) * LEVELS) + 1.0
            gain = REACH * jnp.exp(level * (-1.0 / LEVELS))
            ret_send[at, 0] = level.astype(I16)
            for block, (f, c, k) in enumerate(blocks):
                value = res_all[f, c, at * per + k]
                ret_send[at, 1 + block] = jnp.round(value * gain[block : block + 1, :]).astype(I16)
        for d in order:
            ret_copy(d, me).start()

    def take_back():
        blocks = [(f, c, k) for f in range(freqs) for c in range(2) for k in range(per)]
        for f, c, k in blocks:
            res_ref[f, k, c, strip(me), :] = res_all[f, c, me * per + k]
        for d in order:
            at = source(d)
            ret_copy(d, at).wait_recv()
            gains = gains_of(ret_recv[at, 0])
            for block, (f, c, k) in enumerate(blocks):
                res_ref[f, k, c, strip(at), :] = (
                    ret_recv[at, 1 + block].astype(F32) * gains[block : block + 1, :]
                )

    def take_use(f, c):
        for d in order:
            use_copy(f, c, d, source(d)).wait_recv()

    def adjoint_terms(f, c, t):
        here = pl.ds(pl.multiple_of(t * TILE, TILE), TILE)
        data = jnp.concatenate(
            [
                jnp.concatenate([adj[f, c, i * SIDE + j] for j in range(SIDE)], axis=1)
                for i in range(SIDE)
            ],
            axis=0,
        )
        by_re = jnp.dot(gd[f, here, :half], data, preferred_element_type=F32)
        by_im = jnp.dot(gd[f, here, half:], data, preferred_element_type=F32)
        rec_re = rd[f, here, :half].astype(F32)
        rec_im = rd[f, here, half:].astype(F32)
        if c == 0:
            terms = rec_re * by_re - rec_im * by_im
        else:
            terms = rec_re * by_im + rec_im * by_re
        result = terms[:, :lanes]
        for at in range(lanes, half, lanes):
            result = result + terms[:, at : at + lanes]
        return here, result

    def adjoint(f, c, start, stop):
        def body(t, carry):
            here, result = adjoint_terms(f, c, t)
            if f + c > 0:
                result = total[here, :] + result
            if f + c < 2:
                total[here, :] = result
                return carry
            sums = [
                jnp.sum(result[b * lanes : (b + 1) * lanes, :].T, axis=0, keepdims=True)
                for b in range(groups)
            ]
            summed[pl.ds(pl.multiple_of(t * groups, groups), groups), :] = jnp.concatenate(sums, 0)
            return carry

        lax.fori_loop(start, stop, body, 0)

    def forward_part(f, start, stop):
        if start == 0:
            acc[...] = jnp.zeros_like(acc)
        forward(f, start, stop)
        if stop == tiles:
            finish_part(f)

    steps = {
        "greet": greet, "tables": take_tables, "obs": give_obs, "take_obs": take_obs,
        "forward": forward_part, "share": share, "reduce": reduce, "back": give_back,
        "use": take_use, "adjoint": adjoint,
    }
    for name, *rest in plan(tiles):
        steps[name](*rest)

    own_rows = grad_ref.shape[0]
    swap = pltpu.make_async_remote_copy(
        src_ref=summed.at[pl.ds(pl.multiple_of((1 - mine_f) * own_rows, own_rows), own_rows)],
        dst_ref=other,
        send_sem=ex_send,
        recv_sem=ex_recv,
        device_id={"freq": 1 - mine_f},
        device_id_type=MESH,
    )
    swap.start()

    take_back()
    for d in order:
        tab_copy(d, me).wait_send()
        obs_copy(d, me).wait_send()
        ret_copy(d, me).wait_send()
        for f in range(freqs):
            for c in range(2):
                sum_copy(f, c, d, me).wait_send()
                use_copy(f, c, d, me).wait_send()
    swap.wait()
    mine = summed[pl.ds(pl.multiple_of(mine_f * own_rows, own_rows), own_rows), :]
    grad_ref[...] = mine + other[...]


def grid_plan(tiles):
    return [
        ("forward", 0, 0, 1), ("greet",), ("obs",), ("forward", 0, 1, tiles), ("share", 0),
        ("forward", 1, 0, tiles // 2), ("tables",), ("take_obs",), ("forward", 1, tiles // 2, tiles),
        ("share", 1), ("reduce", 0, 0), ("reduce", 0, 1),
        ("use", 0, 0), ("adjoint", 0, 0, 0, tiles), ("reduce", 1, 0),
        ("use", 0, 1), ("adjoint", 0, 1, 0, tiles), ("reduce", 1, 1), ("back",),
        ("use", 1, 0), ("adjoint", 1, 0, 0, tiles), ("use", 1, 1), ("adjoint", 1, 1, 0, tiles),
    ]


def ring_kernel(n, snake, st_ref, rt_ref, refl_ref, g_hbm, r_hbm, obs_ref, grad_ref, res_ref,
           raw, g32, r32, gd, rd, scaled, acc, part, first, held, gath_a, gath_b, gath_c, gath_d, adj, total, summed, other,
           raw_sem, rs_send, rs_recv, ag_send, ag_recv, ex_send, ex_recv):
    per = obs_ref.shape[1]
    lanes = obs_ref.shape[3]
    freqs, points, wide = gd.shape
    half = wide // 2
    tiles = points // TILE
    groups = TILE // lanes
    pairs = SIDE * SIDE
    gath = ((gath_a, gath_b), (gath_c, gath_d))
    me = lax.axis_index("slab")
    mine_f = lax.axis_index("freq")

    def index_of(pos):
        if not snake:
            return pos
        return 2 * pos + (pos // (n // 2)) * (2 * n - 1 - 4 * pos)

    place = me // 2 + (me % 2) * (n - 1 - 2 * (me // 2)) if snake else me
    ways = (1, -1)
    targets = tuple(index_of((place + way + n) % n) for way in ways)
    low = (n - 1) // 2
    high = n - 1 - low

    barrier = pltpu.get_barrier_semaphore()
    for target in targets:
        pl.semaphore_signal(barrier, inc=1, device_id={"slab": target}, device_id_type=MESH)
    pl.semaphore_signal(barrier, inc=1, device_id={"freq": 1 - mine_f}, device_id_type=MESH)

    def fetches(q, slot):
        return (
            pltpu.make_async_copy(g_hbm.at[q], raw.at[slot, 0], raw_sem.at[slot, 0]),
            pltpu.make_async_copy(r_hbm.at[q], raw.at[slot, 1], raw_sem.at[slot, 1]),
        )

    for q in range(2):
        for copy in fetches(q, q):
            copy.start()

    def forward_tile(f, t):
        q = f * tiles + t
        slot = q % 2
        for copy in fetches(q, slot):
            copy.wait()
        g32[...] = raw[slot, 0].astype(F32)
        r32[...] = raw[slot, 1].astype(F32)

        @pl.when(q + 2 < freqs * tiles)
        def _():
            for copy in fetches(q + 2, slot):
                copy.start()

        refl = refl_ref[pl.ds(pl.multiple_of(t * groups, groups), groups), :]
        weight = jnp.concatenate(
            [jnp.broadcast_to(refl[b : b + 1, :], (lanes, lanes)).T for b in range(groups)], axis=0
        )
        here = pl.ds(pl.multiple_of(t * TILE, TILE), TILE)
        for block in range(SIDE):
            for comp in range(2):
                rows = pl.ds(block * 2 + comp, TILE, stride=2 * SIDE)
                cols = slice(comp * half + block * lanes, comp * half + (block + 1) * lanes)
                green = g32[rows, :]
                gd[f, here, cols] = green.astype(BF16)
                scaled[:, cols] = (green * weight).astype(BF16)
                rd[f, here, cols] = r32[rows, :].astype(BF16)
        prod = lax.dot_general(
            scaled[...], rd[f, here, :], (((0,), (0,)), ((), ())), preferred_element_type=F32
        )
        acc[...] += prod

    def forward(f, start, stop):
        def body(t, carry):
            forward_tile(f, t)
            return carry

        lax.fori_loop(start, stop, body, 0)

    def squares(i, j):
        s_re = slice(i * lanes, (i + 1) * lanes)
        s_im = slice(half + i * lanes, half + (i + 1) * lanes)
        r_re = slice(j * lanes, (j + 1) * lanes)
        r_im = slice(half + j * lanes, half + (j + 1) * lanes)
        return s_re, s_im, r_re, r_im

    def finish_part(f):
        for k in range(pairs):
            s_re, s_im, r_re, r_im = squares(k // SIDE, k % SIDE)
            part[f, k, 0] = acc[s_re, r_re] - acc[s_im, r_im]
            part[f, k, 1] = acc[s_re, r_im] + acc[s_im, r_re]
        part[f, pairs] = jnp.zeros((2, lanes, lanes), F32)

    def hops(f, w):
        return high if f == w else low

    lanes_of = [(c, w) for c in range(2) for w in range(2)]

    def held_at(panel):
        sb = panel // RB
        rb = panel % RB
        i = jnp.where(st_ref[0, 0] == sb, 0, jnp.where(st_ref[0, 1] == sb, SIDE, 2 * pairs))
        j = jnp.where(rt_ref[0, 0] == rb, 0, jnp.where(rt_ref[0, 1] == rb, 1, 2 * pairs))
        return jnp.minimum(i + j, pairs)

    def own(f, c, w, away):
        owner = index_of((place + ways[w] * away + n) % n)
        return [part[f, held_at(owner * per + k), c] for k in range(per)]

    def rs_copy(f, c, w, src, step):
        return pltpu.make_async_remote_copy(
            src_ref=src,
            dst_ref=held.at[f, c, w, step],
            send_sem=rs_send.at[f, c, w, step],
            recv_sem=rs_recv.at[f, c, w, step],
            device_id={"slab": targets[w]},
            device_id_type=MESH,
        )

    def ag_copy(f, c, w, step, away):
        owner = index_of((place - ways[w] * away + n) % n)
        view = gath[f][c].at[pl.ds(owner * per, per)]
        return pltpu.make_async_remote_copy(
            src_ref=view,
            dst_ref=view,
            send_sem=ag_send.at[f, c, w, step],
            recv_sem=ag_recv.at[f, c, w, step],
            device_id={"slab": targets[w]},
            device_id_type=MESH,
        )

    def rs_start(f):
        for c, w in lanes_of:
            mine = own(f, c, w, hops(f, w))
            for k in range(per):
                first[f, c, w, k] = mine[k]
            rs_copy(f, c, w, first.at[f, c, w], 0).start()

    def rs_pass(f, step, only=None):
        for c, w in lanes_of:
            if only is not None and w != only:
                continue
            rs_copy(f, c, w, held.at[f, c, w, step], step).wait_recv()
            mine = own(f, c, w, hops(f, w) - step - 1)
            for k in range(per):
                held[f, c, w, step, k] = held[f, c, w, step, k] + mine[k]
            rs_copy(f, c, w, held.at[f, c, w, step], step + 1).start()

    def ag_pass(f, step, only=None):
        for c, w in lanes_of:
            if only is not None and w != only:
                continue
            ag_copy(f, c, w, step, step + 1).wait_recv()
            ag_copy(f, c, w, step + 1, step + 1).start()

    def rs_longer(f):
        if high > low:
            rs_pass(f, high - 2, f)

    def ag_longer(f):
        if high > low:
            ag_pass(f, high - 2, f)

    def rs_finish(f):
        for c in range(2):
            for w in range(2):
                last = hops(f, w) - 1
                rs_copy(f, c, w, held.at[f, c, w, last], last).wait_recv()
            mine = own(f, c, 0, 0)
            for k in range(per):
                value = (
                    held[f, c, 0, hops(f, 0) - 1, k] + held[f, c, 1, hops(f, 1) - 1, k] + mine[k]
                ) - obs_ref[f, k, c]
                res_ref[f, k, c] = value
                gath[f][c][me * per + k] = value.astype(BF16)
            for w in range(2):
                ag_copy(f, c, w, 0, 0).start()

    def ag_finish(f, c):
        for w in range(2):
            last = hops(f, w) - 1
            ag_copy(f, c, w, last, last + 1).wait_recv()
        for k in range(pairs):
            i, j = k // SIDE, k % SIDE
            panel = st_ref[0, i] * RB + rt_ref[0, j]
            s_re, s_im, r_re, r_im = squares(i, j)
            adj[f, c, s_re, r_re] = gath[f][c][panel]

    def adjoint_terms(f, c, t):
        here = pl.ds(pl.multiple_of(t * TILE, TILE), TILE)
        data = adj[f, c]
        by_re = jnp.dot(gd[f, here, :half], data, preferred_element_type=F32)
        by_im = jnp.dot(gd[f, here, half:], data, preferred_element_type=F32)
        rec_re = rd[f, here, :half].astype(F32)
        rec_im = rd[f, here, half:].astype(F32)
        if c == 0:
            terms = rec_re * by_re - rec_im * by_im
        else:
            terms = rec_re * by_im + rec_im * by_re
        result = terms[:, :lanes]
        for at in range(lanes, half, lanes):
            result = result + terms[:, at : at + lanes]
        return here, result

    def adjoint(f, c):
        def body(t, carry):
            here, result = adjoint_terms(f, c, t)
            if f + c > 0:
                result = total[here, :] + result
            if f + c < 2:
                total[here, :] = result
                return carry
            rows = [
                jnp.sum(result[b * lanes : (b + 1) * lanes, :].T, axis=0, keepdims=True)
                for b in range(groups)
            ]
            summed[pl.ds(pl.multiple_of(t * groups, groups), groups), :] = jnp.concatenate(rows, 0)
            return carry

        lax.fori_loop(0, tiles, body, 0)

    acc[...] = jnp.zeros_like(acc)
    forward(0, 0, tiles)
    finish_part(0)
    pl.semaphore_wait(barrier, 3)
    rs_start(0)
    acc[...] = jnp.zeros_like(acc)
    forward(1, 0, tiles // 2)
    rs_pass(0, 0)
    forward(1, tiles // 2, tiles)
    finish_part(1)
    rs_start(1)

    def rs_both(step, carry):
        rs_pass(0, step)
        rs_pass(1, step - 1)
        return carry

    lax.fori_loop(1, low - 1, rs_both, 0)
    rs_longer(0)
    rs_pass(1, low - 2)
    rs_finish(0)
    rs_longer(1)
    ag_pass(0, 0)
    rs_finish(1)

    def ag_both(step, carry):
        ag_pass(0, step)
        ag_pass(1, step - 1)
        return carry

    lax.fori_loop(1, low - 1, ag_both, 0)
    ag_longer(0)
    ag_pass(1, low - 2)
    ag_finish(0, 0)
    adjoint(0, 0)
    ag_longer(1)
    ag_finish(0, 1)
    adjoint(0, 1)
    ag_finish(1, 0)
    adjoint(1, 0)
    ag_finish(1, 1)
    adjoint(1, 1)

    own_rows = grad_ref.shape[0]
    swap = pltpu.make_async_remote_copy(
        src_ref=summed.at[pl.ds(pl.multiple_of((1 - mine_f) * own_rows, own_rows), own_rows)],
        dst_ref=other,
        send_sem=ex_send,
        recv_sem=ex_recv,
        device_id={"freq": 1 - mine_f},
        device_id_type=MESH,
    )
    swap.start()

    def drain(step, carry):
        for f in range(2):
            for c, w in lanes_of:
                rs_copy(f, c, w, first.at[f, c, w], step).wait_send()
                ag_copy(f, c, w, step, step).wait_send()
        return carry

    lax.fori_loop(0, low, drain, 0)
    if high > low:
        for f in range(2):
            for c in range(2):
                rs_copy(f, c, f, first.at[f, c, f], high - 1).wait_send()
                ag_copy(f, c, f, high - 1, high - 1).wait_send()
    swap.wait()
    mine = summed[pl.ds(pl.multiple_of(mine_f * own_rows, own_rows), own_rows), :]
    grad_ref[...] = mine + other[...]


def interleaved_tiles(green, lanes):
    freqs, points, comps, width = green.shape
    view = green.reshape(freqs, points, comps, width // lanes, lanes).transpose(0, 1, 3, 2, 4)
    tiles = freqs * points // TILE
    return view.reshape(tiles, TILE * comps * width // lanes, lanes)


def grid_on_device(reflectivity, source_green, receiver_green, observed, source_table, receiver_table):
    freqs, points, comps, width = source_green.shape
    per = observed.shape[1]
    lanes = observed.shape[3]
    pairs = SIDE * SIDE
    n = lanes // STRIP
    panels = n * per
    blocks = 2 * pairs + 1
    wide = comps * width
    tall = TILE * wide // lanes
    lines = points // lanes
    vmem = pl.BlockSpec(memory_space=pltpu.VMEM)
    smem = pl.BlockSpec(memory_space=pltpu.SMEM)
    hbm = pl.BlockSpec(memory_space=pl.ANY)
    sem = pltpu.SemaphoreType.DMA

    def codes(*shape):
        return pltpu.VMEM(shape + (STRIP, lanes), I16)

    gradient, residual = pl.pallas_call(
        functools.partial(grid_kernel, grid_plan),
        in_specs=[smem, smem, vmem, hbm, hbm, vmem],
        out_specs=[vmem, vmem],
        out_shape=[
            jax.ShapeDtypeStruct((lines // 2, lanes), F32),
            jax.ShapeDtypeStruct(observed.shape, F32),
        ],
        scratch_shapes=[
            pltpu.VMEM((2, 2, tall, lanes), BF16),
            pltpu.VMEM((tall, lanes), F32),
            pltpu.VMEM((tall, lanes), F32),
            pltpu.VMEM((freqs, points, wide), BF16),
            pltpu.VMEM((freqs, points, wide), BF16),
            pltpu.VMEM((TILE, wide), BF16),
            pltpu.VMEM((wide, wide), F32),
            pltpu.VMEM((freqs, pairs, 2, lanes, lanes), F32),
            pltpu.VMEM((freqs, 2, pairs, lanes, lanes), BF16),
            pltpu.VMEM((points, lanes), F32),
            pltpu.VMEM((lines, lanes), F32),
            pltpu.VMEM((lines // 2, lanes), F32),
            pltpu.VMEM((8, 128), jnp.int32),
            pltpu.VMEM((n, 8, 128), jnp.int32),
            pltpu.SMEM((n, 8, 128), jnp.int32),
            codes(n, blocks), codes(n, blocks),
            pltpu.VMEM((freqs, 2, panels, STRIP, lanes), F32),
            codes(freqs, n, blocks), codes(freqs, n, blocks),
            pltpu.VMEM((n, pairs + 1, STRIP, lanes), F32),
            pltpu.VMEM((freqs, 2, panels, STRIP, lanes), F32),
            pltpu.VMEM((panels, STRIP, lanes), BF16),
            pltpu.VMEM((freqs, 2, n, pairs, STRIP, lanes), BF16),
            codes(n, blocks), codes(n, blocks),
            sem((2, 2)),
            sem((n,)), sem((n,)), sem,
            sem((n,)), sem((n,)),
            sem((freqs, 2, n)), sem((freqs, 2, n)),
            sem((freqs, 2, n)), sem((freqs, 2, n)),
            sem((n,)), sem((n,)),
            sem, sem,
        ],
        compiler_params=pltpu.CompilerParams(
            collective_id=0, has_side_effects=True, vmem_limit_bytes=VMEM_BYTES
        ),
        name="migration",
    )(
        source_table,
        receiver_table,
        reflectivity.reshape(lines, lanes),
        interleaved_tiles(source_green, lanes),
        interleaved_tiles(receiver_green, lanes),
        observed,
    )
    return gradient.reshape(points // 2), residual


def ring_on_device(reflectivity, source_green, receiver_green, observed, source_table, receiver_table):
    freqs, points, comps, width = source_green.shape
    per = observed.shape[1]
    lanes = observed.shape[3]
    n = lax.axis_size("slab")
    pairs = SIDE * SIDE
    wide = comps * width
    tall = TILE * wide // lanes
    rows = points // lanes
    vmem = pl.BlockSpec(memory_space=pltpu.VMEM)
    smem = pl.BlockSpec(memory_space=pltpu.SMEM)
    hbm = pl.BlockSpec(memory_space=pl.ANY)
    hop_sems = pltpu.SemaphoreType.DMA((freqs, 2, 2, n // 2))
    gradient, residual = pl.pallas_call(
        functools.partial(ring_kernel, n, n == 8),
        in_specs=[smem, smem, vmem, hbm, hbm, vmem],
        out_specs=[vmem, vmem],
        out_shape=[
            jax.ShapeDtypeStruct((rows // 2, lanes), F32),
            jax.ShapeDtypeStruct(observed.shape, F32),
        ],
        scratch_shapes=[
            pltpu.VMEM((2, 2, tall, lanes), BF16),
            pltpu.VMEM((tall, lanes), F32),
            pltpu.VMEM((tall, lanes), F32),
            pltpu.VMEM((freqs, points, wide), BF16),
            pltpu.VMEM((freqs, points, wide), BF16),
            pltpu.VMEM((TILE, wide), BF16),
            pltpu.VMEM((wide, wide), F32),
            pltpu.VMEM((freqs, pairs + 1, 2, lanes, lanes), F32),
            pltpu.VMEM((freqs, 2, 2, per, lanes, lanes), F32),
            pltpu.VMEM((freqs, 2, 2, n // 2, per, lanes, lanes), F32),
            pltpu.VMEM((n * per, lanes, lanes), BF16),
            pltpu.VMEM((n * per, lanes, lanes), BF16),
            pltpu.VMEM((n * per, lanes, lanes), BF16),
            pltpu.VMEM((n * per, lanes, lanes), BF16),
            pltpu.VMEM((freqs, 2, width, width), BF16),
            pltpu.VMEM((points, lanes), F32),
            pltpu.VMEM((rows, lanes), F32),
            pltpu.VMEM((rows // 2, lanes), F32),
            pltpu.SemaphoreType.DMA((2, 2)),
            hop_sems,
            hop_sems,
            hop_sems,
            hop_sems,
            pltpu.SemaphoreType.DMA,
            pltpu.SemaphoreType.DMA,
        ],
        compiler_params=pltpu.CompilerParams(collective_id=0, has_side_effects=True, vmem_limit_bytes=VMEM_BYTES),
        name="migration",
    )(
        source_table,
        receiver_table,
        reflectivity.reshape(rows, lanes),
        interleaved_tiles(source_green, lanes),
        interleaved_tiles(receiver_green, lanes),
        observed,
    )
    return gradient.reshape(points // 2), residual


def solution(mesh):
    on_device = grid_on_device if mesh.shape["slab"] == SLICES else ring_on_device
    return jax.shard_map(
        on_device,
        mesh=mesh,
        in_specs=(
            P(("parts", "slab")),
            P("freq", ("parts", "slab"), None, None),
            P("freq", ("parts", "slab"), None, None),
            P("freq", ("parts", "slab"), None, None, None),
            P(("parts", "slab"), None),
            P(("parts", "slab"), None),
        ),
        out_specs=(P(("parts", "slab", "freq")), P("freq", ("parts", "slab"), None, None, None)),
        check_vma=False,
    )
```

```python
import functools

import jax
import jax.numpy as jnp
from jax import lax
from jax.experimental import pallas as pl
from jax.experimental.pallas import tpu as pltpu
from jax.sharding import PartitionSpec as P

RB = 4
TILE = 1024
SIDE = 2
MESH = pl.DeviceIdType.MESH
F32 = jnp.float32
BF16 = jnp.bfloat16
I16 = jnp.int16
STRIP = 16
SLICES = 8
REACH = 32600.0
VMEM_BYTES = 56 * 2**20


def hand_over(grad_in, res_in, grad_out, res_out, sems):
    copies = [
        pltpu.make_async_copy(grad_in, grad_out, sems.at[0]),
        pltpu.make_async_copy(res_in, res_out, sems.at[1]),
    ]
    for copy in copies:
        copy.start()
    for copy in copies:
        copy.wait()


def unit_of(values):
    peak = functools.reduce(
        jnp.maximum, [jnp.max(jnp.abs(value), axis=0, keepdims=True) for value in values]
    )
    return jnp.maximum(peak, 1e-30) * (1.0 / REACH)


def grid_kernel(plan, st_ref, rt_ref, refl_ref, g_hbm, r_hbm, obs_ref, grad_ref, res_ref,
                obs, refl_own, raw, g32, r32, gd, rd, scaled_a, acc, part, adj, total, summed, other,
                tab_send, tab_recv, tab, unit_send, unit_recv, obs_send, obs_recv, obs_all, sum_send, sum_recv,
                terms, res_all, rounded, use_send, ret_send, ret_recv,
                in_sem, raw_sem, unit_ss, unit_rs, tab_ss, tab_rs, tab_local, obs_ss, obs_rs, sum_ss, sum_rs, use_ss, use_rs,
                ret_ss, ret_rs, ex_send, ex_recv):
    per = obs.shape[1]
    lanes = obs.shape[3]
    freqs, points, wide = gd.shape
    half = wide // 2
    tiles = points // TILE
    groups = TILE // lanes
    pairs = SIDE * SIDE
    n = lanes // STRIP
    panels = n * per
    me = lax.axis_index("slab")
    mine_f = lax.axis_index("freq")
    order = sorted(range(1, n), key=lambda d: abs(d - n // 2))

    def to(d):
        return lax.rem(me + d, n)

    def source(d):
        return lax.rem(me + n - d, n)

    def strip(at):
        return pl.ds(pl.multiple_of(at * STRIP, STRIP), STRIP)

    barrier = pltpu.get_barrier_semaphore()
    for d in order:
        pl.semaphore_signal(barrier, inc=1, device_id={"slab": to(d)}, device_id_type=MESH)
    pl.semaphore_signal(barrier, inc=1, device_id={"freq": 1 - mine_f}, device_id_type=MESH)

    def fetches(q, slot):
        return (
            pltpu.make_async_copy(g_hbm.at[q], raw.at[slot, 0], raw_sem.at[slot, 0]),
            pltpu.make_async_copy(r_hbm.at[q], raw.at[slot, 1], raw_sem.at[slot, 1]),
        )

    obs_load = pltpu.make_async_copy(obs_ref, obs, in_sem.at[0])
    refl_load = pltpu.make_async_copy(refl_ref, refl_own, in_sem.at[1])
    obs_load.start()
    refl_load.start()
    for q in range(2):
        for copy in fetches(q, q):
            copy.start()

    lane = lax.broadcasted_iota(jnp.int32, tab_send.shape, 1)
    line = jnp.zeros(tab_send.shape, jnp.int32)
    for at, value in enumerate((st_ref[0, 0], st_ref[0, 1], rt_ref[0, 0], rt_ref[0, 1])):
        line = jnp.where(lane == at, value, line)
    tab_send[...] = line
    tab_recv[me] = line
    terms[:, pairs] = jnp.zeros((n, STRIP, lanes), F32)

    def shape_tile(q):
        f, t = q // tiles, q % tiles
        slot = q % 2
        for copy in fetches(q, slot):
            copy.wait()
        g32[...] = raw[slot, 0].astype(F32)
        r32[...] = raw[slot, 1].astype(F32)

        @pl.when(q + 2 < freqs * tiles)
        def _():
            for copy in fetches(q + 2, slot):
                copy.start()

        refl = refl_own[pl.ds(pl.multiple_of(t * groups, groups), groups), :]
        weight = jnp.concatenate(
            [jnp.broadcast_to(refl[b : b + 1, :], (lanes, lanes)).T for b in range(groups)], axis=0
        )
        here = pl.ds(pl.multiple_of(t * TILE, TILE), TILE)
        for block in range(SIDE):
            for comp in range(2):
                lines = pl.ds(block * 2 + comp, TILE, stride=2 * SIDE)
                cols = slice(comp * half + block * lanes, comp * half + (block + 1) * lanes)
                green = g32[lines, :]
                gd[f, here, cols] = green.astype(BF16)
                scaled_a[:, cols] = (green * weight).astype(BF16)
                rd[f, here, cols] = r32[lines, :].astype(BF16)

    def sum_tile(q):
        f, t = q // tiles, q % tiles
        here = pl.ds(pl.multiple_of(t * TILE, TILE), TILE)
        acc[...] += lax.dot_general(
            scaled_a[...], rd[f, here, :], (((0,), (0,)), ((), ())), preferred_element_type=F32
        )

    def forward(start, stop):
        def body(q, carry):
            shape_tile(q)
            sum_tile(q)
            return carry

        lax.fori_loop(start, stop, body, 0)

    def clear():
        acc[...] = jnp.zeros_like(acc)

    def squares(i, j):
        s_re = slice(i * lanes, (i + 1) * lanes)
        s_im = slice(half + i * lanes, half + (i + 1) * lanes)
        r_re = slice(j * lanes, (j + 1) * lanes)
        r_im = slice(half + j * lanes, half + (j + 1) * lanes)
        return s_re, s_im, r_re, r_im

    def finish_part(f):
        for k in range(pairs):
            s_re, s_im, r_re, r_im = squares(k // SIDE, k % SIDE)
            part[f, k, 0] = acc[s_re, r_re] - acc[s_im, r_im]
            part[f, k, 1] = acc[s_re, r_im] + acc[s_im, r_re]

    def remote(src, dst, send, recv, d):
        return pltpu.make_async_remote_copy(
            src_ref=src, dst_ref=dst, send_sem=send, recv_sem=recv,
            device_id={"slab": to(d)}, device_id_type=MESH,
        )

    def tab_copy(d, at):
        return remote(tab_send, tab_recv.at[at], tab_ss.at[d], tab_rs.at[d], d)

    def unit_copy(kind, d, at):
        return remote(
            unit_send.at[kind], unit_recv.at[kind, at], unit_ss.at[kind, d], unit_rs.at[kind, d], d
        )

    def obs_copy(d, at):
        return remote(obs_send.at[to(d)], obs_recv.at[at], obs_ss.at[d], obs_rs.at[d], d)

    def sum_copy(f, c, d, at):
        part_of = pl.ds(c * pairs, pairs)
        return remote(
            sum_send.at[f, to(d), part_of], sum_recv.at[f, at, part_of],
            sum_ss.at[f, c, d], sum_rs.at[f, c, d], d,
        )

    def use_copy(f, c, d, at):
        return remote(
            use_send.at[f, c, to(d)], adj.at[f, c, :, strip(at), :],
            use_ss.at[f, c, d], use_rs.at[f, c, d], d,
        )

    def ret_copy(d, at):
        return remote(ret_send.at[to(d)], ret_recv.at[at], ret_ss.at[d], ret_rs.at[d], d)

    def encode(kind, values, out):
        unit = unit_of(values)
        unit_send[kind] = unit
        gain = 1.0 / unit
        for at, value in enumerate(values):
            code = jnp.round(value * gain).astype(I16)
            out[:, at] = code.reshape(n, STRIP, lanes)

    fcks = [(f, c, k) for f in range(freqs) for c in range(2) for k in range(per)]

    def greet():
        obs_load.wait()
        refl_load.wait()
        encode(freqs, [obs[f, k, c] for f, c, k in fcks], obs_send)
        pl.semaphore_wait(barrier, n)
        for d in order:
            tab_copy(d, me).start()
            unit_copy(freqs, d, me).start()
            obs_copy(d, me).start()

    def take_tables():
        for d in order:
            tab_copy(d, source(d)).wait_recv()
        copy = pltpu.make_async_copy(tab_recv, tab, tab_local)
        copy.start()
        copy.wait()

    def take_obs():
        for d in order:
            at = source(d)
            unit_copy(freqs, d, at).wait_recv()
            obs_copy(d, at).wait_recv()
            unit = unit_recv[freqs, at]
            for block, (f, c, k) in enumerate(fcks):
                obs_all[f, c, at * per + k] = obs_recv[at, block].astype(F32) * unit
        for f, c, k in fcks:
            obs_all[f, c, me * per + k] = obs[f, k, c, strip(me), :]

    def share(f):
        encode(f, [part[f, b, c] for c in range(2) for b in range(pairs)], sum_send.at[f])
        for d in order:
            unit_copy(f, d, me).start()
            sum_copy(f, 0, d, me).start()
        for d in order:
            sum_copy(f, 1, d, me).start()

    def tables():
        return [tuple(tab[s, 0, at] for at in range(4)) for s in range(n)]

    def reduce(f, c):
        for b in range(pairs):
            terms[me, b] = part[f, b, c, strip(me), :]
        for d in order:
            at = source(d)
            if c == 0:
                unit_copy(f, d, at).wait_recv()
            sum_copy(f, c, d, at).wait_recv()
            unit = unit_recv[f, at]
            for b in range(pairs):
                terms[at, b] = sum_recv[f, at, c * pairs + b].astype(F32) * unit
        rows_of, cols_of = [], []
        for table in tables():
            rows_of.append([
                jnp.where(table[0] == sb, 0, jnp.where(table[1] == sb, SIDE, pairs))
                for sb in range(panels // RB)
            ])
            cols_of.append([
                jnp.where(table[2] == rb, 0, jnp.where(table[3] == rb, 1, pairs)) for rb in range(RB)
            ])
        for panel in range(panels):
            value = -obs_all[f, c, panel]
            for s in range(n):
                index = jnp.minimum(rows_of[s][panel // RB] + cols_of[s][panel % RB], pairs)
                value = value + terms[s, index]
            res_all[f, c, panel] = value
            rounded[panel] = value.astype(BF16)
        for at, table in enumerate(tables()):
            for b in range(pairs):
                use_send[f, c, at, b] = rounded[table[b // SIDE] * RB + table[2 + b % SIDE]]
        for d in order:
            use_copy(f, c, d, me).start()
        for b in range(pairs):
            adj[f, c, b, strip(me), :] = use_send[f, c, me, b]

    def give_back():
        unit = unit_of([res_all[f, c, p] for f in range(freqs) for c in range(2) for p in range(panels)])
        unit_send[freqs + 1] = unit
        gain = 1.0 / unit
        for at in range(n):
            for block, (f, c, k) in enumerate(fcks):
                ret_send[at, block] = jnp.round(res_all[f, c, at * per + k] * gain).astype(I16)
        for d in order:
            unit_copy(freqs + 1, d, me).start()
            ret_copy(d, me).start()

    def take_back():
        for f, c, k in fcks:
            res_ref[f, k, c, strip(me), :] = res_all[f, c, me * per + k]
        for d in order:
            at = source(d)
            unit_copy(freqs + 1, d, at).wait_recv()
            ret_copy(d, at).wait_recv()
            unit = unit_recv[freqs + 1, at]
            for block, (f, c, k) in enumerate(fcks):
                res_ref[f, k, c, strip(at), :] = ret_recv[at, block].astype(F32) * unit

    def take_use(f, c):
        for d in order:
            use_copy(f, c, d, source(d)).wait_recv()

    def adjoint_terms(f, c, t):
        here = pl.ds(pl.multiple_of(t * TILE, TILE), TILE)
        data = jnp.concatenate(
            [
                jnp.concatenate([adj[f, c, i * SIDE + j] for j in range(SIDE)], axis=1)
                for i in range(SIDE)
            ],
            axis=0,
        )
        by_re = jnp.dot(gd[f, here, :half], data, preferred_element_type=F32)
        by_im = jnp.dot(gd[f, here, half:], data, preferred_element_type=F32)
        rec_re = rd[f, here, :half].astype(F32)
        rec_im = rd[f, here, half:].astype(F32)
        if c == 0:
            terms = rec_re * by_re - rec_im * by_im
        else:
            terms = rec_re * by_im + rec_im * by_re
        result = terms[:, :lanes]
        for at in range(lanes, half, lanes):
            result = result + terms[:, at : at + lanes]
        return here, result

    def adjoint(f, c, start, stop):
        def body(t, carry):
            here, result = adjoint_terms(f, c, t)
            if f + c > 0:
                result = total[here, :] + result
            if f + c < 2:
                total[here, :] = result
                return carry
            sums = [
                jnp.sum(result[b * lanes : (b + 1) * lanes, :].T, axis=0, keepdims=True)
                for b in range(groups)
            ]
            summed[pl.ds(pl.multiple_of(t * groups, groups), groups), :] = jnp.concatenate(sums, 0)
            return carry

        lax.fori_loop(start, stop, body, 0)

    steps = {
        "greet": greet, "tables": take_tables, "take_obs": take_obs,
        "shape": shape_tile, "sum": sum_tile, "forward": forward, "clear": clear, "part": finish_part, "share": share, "reduce": reduce, "back": give_back,
        "use": take_use, "adjoint": adjoint,
    }
    for name, *rest in plan(tiles):
        steps[name](*rest)

    own_rows = grad_ref.shape[0]
    swap = pltpu.make_async_remote_copy(
        src_ref=summed.at[pl.ds(pl.multiple_of((1 - mine_f) * own_rows, own_rows), own_rows)],
        dst_ref=other,
        send_sem=ex_send,
        recv_sem=ex_recv,
        device_id={"freq": 1 - mine_f},
        device_id_type=MESH,
    )
    swap.start()

    take_back()
    for d in order:
        tab_copy(d, me).wait_send()
        obs_copy(d, me).wait_send()
        ret_copy(d, me).wait_send()
        for kind in range(freqs + 2):
            unit_copy(kind, d, me).wait_send()
        for f in range(freqs):
            for c in range(2):
                sum_copy(f, c, d, me).wait_send()
                use_copy(f, c, d, me).wait_send()
    swap.wait()
    mine = summed[pl.ds(pl.multiple_of(mine_f * own_rows, own_rows), own_rows), :]
    grad_ref[...] = mine + other[...]


def grid_plan(tiles):
    plan = [("greet",), ("clear",), ("forward", 0, tiles), ("part", 0), ("share", 0), ("clear",)]
    plan += [("forward", tiles, tiles + tiles // 2), ("tables",), ("take_obs",)]
    plan += [("forward", tiles + tiles // 2, 2 * tiles), ("part", 1), ("share", 1)]
    plan += [("reduce", f, c) for f in range(2) for c in range(2)]
    plan += [("back",)]
    for f in range(2):
        for c in range(2):
            plan += [("use", f, c), ("adjoint", f, c, 0, tiles)]
    return plan


def ring_kernel(n, snake, st_ref, rt_ref, refl_ref, g_hbm, r_hbm, obs_ref, grad_ref, res_ref,
           raw, g32, r32, gd, rd, scaled, acc, part, first, held, gath_a, gath_b, gath_c, gath_d, adj, total, summed, other,
           raw_sem, rs_send, rs_recv, ag_send, ag_recv, ex_send, ex_recv):
    per = obs_ref.shape[1]
    lanes = obs_ref.shape[3]
    freqs, points, wide = gd.shape
    half = wide // 2
    tiles = points // TILE
    groups = TILE // lanes
    pairs = SIDE * SIDE
    gath = ((gath_a, gath_b), (gath_c, gath_d))
    me = lax.axis_index("slab")
    mine_f = lax.axis_index("freq")

    def index_of(pos):
        if not snake:
            return pos
        return 2 * pos + (pos // (n // 2)) * (2 * n - 1 - 4 * pos)

    place = me // 2 + (me % 2) * (n - 1 - 2 * (me // 2)) if snake else me
    ways = (1, -1)
    targets = tuple(index_of((place + way + n) % n) for way in ways)
    low = (n - 1) // 2
    high = n - 1 - low

    barrier = pltpu.get_barrier_semaphore()
    for target in targets:
        pl.semaphore_signal(barrier, inc=1, device_id={"slab": target}, device_id_type=MESH)
    pl.semaphore_signal(barrier, inc=1, device_id={"freq": 1 - mine_f}, device_id_type=MESH)

    def fetches(q, slot):
        return (
            pltpu.make_async_copy(g_hbm.at[q], raw.at[slot, 0], raw_sem.at[slot, 0]),
            pltpu.make_async_copy(r_hbm.at[q], raw.at[slot, 1], raw_sem.at[slot, 1]),
        )

    for q in range(2):
        for copy in fetches(q, q):
            copy.start()

    def forward_tile(f, t):
        q = f * tiles + t
        slot = q % 2
        for copy in fetches(q, slot):
            copy.wait()
        g32[...] = raw[slot, 0].astype(F32)
        r32[...] = raw[slot, 1].astype(F32)

        @pl.when(q + 2 < freqs * tiles)
        def _():
            for copy in fetches(q + 2, slot):
                copy.start()

        refl = refl_ref[pl.ds(pl.multiple_of(t * groups, groups), groups), :]
        weight = jnp.concatenate(
            [jnp.broadcast_to(refl[b : b + 1, :], (lanes, lanes)).T for b in range(groups)], axis=0
        )
        here = pl.ds(pl.multiple_of(t * TILE, TILE), TILE)
        for block in range(SIDE):
            for comp in range(2):
                rows = pl.ds(block * 2 + comp, TILE, stride=2 * SIDE)
                cols = slice(comp * half + block * lanes, comp * half + (block + 1) * lanes)
                green = g32[rows, :]
                gd[f, here, cols] = green.astype(BF16)
                scaled[:, cols] = (green * weight).astype(BF16)
                rd[f, here, cols] = r32[rows, :].astype(BF16)
        prod = lax.dot_general(
            scaled[...], rd[f, here, :], (((0,), (0,)), ((), ())), preferred_element_type=F32
        )
        acc[...] += prod

    def forward(f, start, stop):
        def body(t, carry):
            forward_tile(f, t)
            return carry

        lax.fori_loop(start, stop, body, 0)

    def squares(i, j):
        s_re = slice(i * lanes, (i + 1) * lanes)
        s_im = slice(half + i * lanes, half + (i + 1) * lanes)
        r_re = slice(j * lanes, (j + 1) * lanes)
        r_im = slice(half + j * lanes, half + (j + 1) * lanes)
        return s_re, s_im, r_re, r_im

    def finish_part(f):
        for k in range(pairs):
            s_re, s_im, r_re, r_im = squares(k // SIDE, k % SIDE)
            part[f, k, 0] = acc[s_re, r_re] - acc[s_im, r_im]
            part[f, k, 1] = acc[s_re, r_im] + acc[s_im, r_re]
        part[f, pairs] = jnp.zeros((2, lanes, lanes), F32)

    def hops(f, w):
        return high if f == w else low

    lanes_of = [(c, w) for c in range(2) for w in range(2)]

    def held_at(panel):
        sb = panel // RB
        rb = panel % RB
        i = jnp.where(st_ref[0, 0] == sb, 0, jnp.where(st_ref[0, 1] == sb, SIDE, 2 * pairs))
        j = jnp.where(rt_ref[0, 0] == rb, 0, jnp.where(rt_ref[0, 1] == rb, 1, 2 * pairs))
        return jnp.minimum(i + j, pairs)

    def own(f, c, w, away):
        owner = index_of((place + ways[w] * away + n) % n)
        return [part[f, held_at(owner * per + k), c] for k in range(per)]

    def rs_copy(f, c, w, src, step):
        return pltpu.make_async_remote_copy(
            src_ref=src,
            dst_ref=held.at[f, c, w, step],
            send_sem=rs_send.at[f, c, w, step],
            recv_sem=rs_recv.at[f, c, w, step],
            device_id={"slab": targets[w]},
            device_id_type=MESH,
        )

    def ag_copy(f, c, w, step, away):
        owner = index_of((place - ways[w] * away + n) % n)
        view = gath[f][c].at[pl.ds(owner * per, per)]
        return pltpu.make_async_remote_copy(
            src_ref=view,
            dst_ref=view,
            send_sem=ag_send.at[f, c, w, step],
            recv_sem=ag_recv.at[f, c, w, step],
            device_id={"slab": targets[w]},
            device_id_type=MESH,
        )

    def rs_start(f):
        for c, w in lanes_of:
            mine = own(f, c, w, hops(f, w))
            for k in range(per):
                first[f, c, w, k] = mine[k]
            rs_copy(f, c, w, first.at[f, c, w], 0).start()

    def rs_pass(f, step, only=None):
        for c, w in lanes_of:
            if only is not None and w != only:
                continue
            rs_copy(f, c, w, held.at[f, c, w, step], step).wait_recv()
            mine = own(f, c, w, hops(f, w) - step - 1)
            for k in range(per):
                held[f, c, w, step, k] = held[f, c, w, step, k] + mine[k]
            rs_copy(f, c, w, held.at[f, c, w, step], step + 1).start()

    def ag_pass(f, step, only=None):
        for c, w in lanes_of:
            if only is not None and w != only:
                continue
            ag_copy(f, c, w, step, step + 1).wait_recv()
            ag_copy(f, c, w, step + 1, step + 1).start()

    def rs_longer(f):
        if high > low:
            rs_pass(f, high - 2, f)

    def ag_longer(f):
        if high > low:
            ag_pass(f, high - 2, f)

    def rs_finish(f):
        for c in range(2):
            for w in range(2):
                last = hops(f, w) - 1
                rs_copy(f, c, w, held.at[f, c, w, last], last).wait_recv()
            mine = own(f, c, 0, 0)
            for k in range(per):
                value = (
                    held[f, c, 0, hops(f, 0) - 1, k] + held[f, c, 1, hops(f, 1) - 1, k] + mine[k]
                ) - obs_ref[f, k, c]
                res_ref[f, k, c] = value
                gath[f][c][me * per + k] = value.astype(BF16)
            for w in range(2):
                ag_copy(f, c, w, 0, 0).start()

    def ag_finish(f, c):
        for w in range(2):
            last = hops(f, w) - 1
            ag_copy(f, c, w, last, last + 1).wait_recv()
        for k in range(pairs):
            i, j = k // SIDE, k % SIDE
            panel = st_ref[0, i] * RB + rt_ref[0, j]
            s_re, s_im, r_re, r_im = squares(i, j)
            adj[f, c, s_re, r_re] = gath[f][c][panel]

    def adjoint_terms(f, c, t):
        here = pl.ds(pl.multiple_of(t * TILE, TILE), TILE)
        data = adj[f, c]
        by_re = jnp.dot(gd[f, here, :half], data, preferred_element_type=F32)
        by_im = jnp.dot(gd[f, here, half:], data, preferred_element_type=F32)
        rec_re = rd[f, here, :half].astype(F32)
        rec_im = rd[f, here, half:].astype(F32)
        if c == 0:
            terms = rec_re * by_re - rec_im * by_im
        else:
            terms = rec_re * by_im + rec_im * by_re
        result = terms[:, :lanes]
        for at in range(lanes, half, lanes):
            result = result + terms[:, at : at + lanes]
        return here, result

    def adjoint(f, c):
        def body(t, carry):
            here, result = adjoint_terms(f, c, t)
            if f + c > 0:
                result = total[here, :] + result
            if f + c < 2:
                total[here, :] = result
                return carry
            rows = [
                jnp.sum(result[b * lanes : (b + 1) * lanes, :].T, axis=0, keepdims=True)
                for b in range(groups)
            ]
            summed[pl.ds(pl.multiple_of(t * groups, groups), groups), :] = jnp.concatenate(rows, 0)
            return carry

        lax.fori_loop(0, tiles, body, 0)

    acc[...] = jnp.zeros_like(acc)
    forward(0, 0, tiles)
    finish_part(0)
    pl.semaphore_wait(barrier, 3)
    rs_start(0)
    acc[...] = jnp.zeros_like(acc)
    forward(1, 0, tiles // 2)
    rs_pass(0, 0)
    forward(1, tiles // 2, tiles)
    finish_part(1)
    rs_start(1)

    def rs_both(step, carry):
        rs_pass(0, step)
        rs_pass(1, step - 1)
        return carry

    lax.fori_loop(1, low - 1, rs_both, 0)
    rs_longer(0)
    rs_pass(1, low - 2)
    rs_finish(0)
    rs_longer(1)
    ag_pass(0, 0)
    rs_finish(1)

    def ag_both(step, carry):
        ag_pass(0, step)
        ag_pass(1, step - 1)
        return carry

    lax.fori_loop(1, low - 1, ag_both, 0)
    ag_longer(0)
    ag_pass(1, low - 2)
    ag_finish(0, 0)
    adjoint(0, 0)
    ag_longer(1)
    ag_finish(0, 1)
    adjoint(0, 1)
    ag_finish(1, 0)
    adjoint(1, 0)
    ag_finish(1, 1)
    adjoint(1, 1)

    own_rows = grad_ref.shape[0]
    swap = pltpu.make_async_remote_copy(
        src_ref=summed.at[pl.ds(pl.multiple_of((1 - mine_f) * own_rows, own_rows), own_rows)],
        dst_ref=other,
        send_sem=ex_send,
        recv_sem=ex_recv,
        device_id={"freq": 1 - mine_f},
        device_id_type=MESH,
    )
    swap.start()

    def drain(step, carry):
        for f in range(2):
            for c, w in lanes_of:
                rs_copy(f, c, w, first.at[f, c, w], step).wait_send()
                ag_copy(f, c, w, step, step).wait_send()
        return carry

    lax.fori_loop(0, low, drain, 0)
    if high > low:
        for f in range(2):
            for c in range(2):
                rs_copy(f, c, f, first.at[f, c, f], high - 1).wait_send()
                ag_copy(f, c, f, high - 1, high - 1).wait_send()
    swap.wait()
    mine = summed[pl.ds(pl.multiple_of(mine_f * own_rows, own_rows), own_rows), :]
    grad_ref[...] = mine + other[...]


def interleaved_tiles(green, lanes):
    freqs, points, comps, width = green.shape
    view = green.reshape(freqs, points, comps, width // lanes, lanes).transpose(0, 1, 3, 2, 4)
    tiles = freqs * points // TILE
    return view.reshape(tiles, TILE * comps * width // lanes, lanes)


def grid_on_device(reflectivity, source_green, receiver_green, observed, source_table, receiver_table):
    freqs, points, comps, width = source_green.shape
    per = observed.shape[1]
    lanes = observed.shape[3]
    pairs = SIDE * SIDE
    n = lanes // STRIP
    panels = n * per
    blocks = 2 * pairs
    wide = comps * width
    tall = TILE * wide // lanes
    lines = points // lanes
    vmem = pl.BlockSpec(memory_space=pltpu.VMEM)
    smem = pl.BlockSpec(memory_space=pltpu.SMEM)
    hbm = pl.BlockSpec(memory_space=pl.ANY)
    sem = pltpu.SemaphoreType.DMA

    def codes(*shape):
        return pltpu.VMEM(shape + (STRIP, lanes), I16)

    gradient, residual = pl.pallas_call(
        functools.partial(grid_kernel, grid_plan),
        in_specs=[smem, smem, hbm, hbm, hbm, hbm],
        out_specs=[vmem, vmem],
        out_shape=[
            jax.ShapeDtypeStruct((lines // 2, lanes), F32),
            jax.ShapeDtypeStruct(observed.shape, F32),
        ],
        scratch_shapes=[
            pltpu.VMEM(observed.shape, F32),
            pltpu.VMEM((lines, lanes), F32),
            pltpu.VMEM((2, 2, tall, lanes), BF16),
            pltpu.VMEM((tall, lanes), F32),
            pltpu.VMEM((tall, lanes), F32),
            pltpu.VMEM((freqs, points, wide), BF16),
            pltpu.VMEM((freqs, points, wide), BF16),
            pltpu.VMEM((TILE, wide), BF16),
            pltpu.VMEM((wide, wide), F32),
            pltpu.VMEM((freqs, pairs, 2, lanes, lanes), F32),
            pltpu.VMEM((freqs, 2, pairs, lanes, lanes), BF16),
            pltpu.VMEM((points, lanes), F32),
            pltpu.VMEM((lines, lanes), F32),
            pltpu.VMEM((lines // 2, lanes), F32),
            pltpu.VMEM((8, 128), jnp.int32),
            pltpu.VMEM((n, 8, 128), jnp.int32),
            pltpu.SMEM((n, 8, 128), jnp.int32),
            pltpu.VMEM((freqs + 2, 1, lanes), F32),
            pltpu.VMEM((freqs + 2, n, 1, lanes), F32),
            codes(n, blocks), codes(n, blocks),
            pltpu.VMEM((freqs, 2, panels, STRIP, lanes), F32),
            codes(freqs, n, blocks), codes(freqs, n, blocks),
            pltpu.VMEM((n, pairs + 1, STRIP, lanes), F32),
            pltpu.VMEM((freqs, 2, panels, STRIP, lanes), F32),
            pltpu.VMEM((panels, STRIP, lanes), BF16),
            pltpu.VMEM((freqs, 2, n, pairs, STRIP, lanes), BF16),
            codes(n, blocks), codes(n, blocks),
            sem((2,)),
            sem((2, 2)),
            sem((freqs + 2, n)), sem((freqs + 2, n)),
            sem((n,)), sem((n,)), sem,
            sem((n,)), sem((n,)),
            sem((freqs, 2, n)), sem((freqs, 2, n)),
            sem((freqs, 2, n)), sem((freqs, 2, n)),
            sem((n,)), sem((n,)),
            sem, sem,
        ],
        compiler_params=pltpu.CompilerParams(
            collective_id=0, has_side_effects=True, vmem_limit_bytes=VMEM_BYTES
        ),
        name="migration",
    )(
        source_table,
        receiver_table,
        reflectivity.reshape(lines, lanes),
        interleaved_tiles(source_green, lanes),
        interleaved_tiles(receiver_green, lanes),
        observed,
    )
    gradient, residual = pl.pallas_call(
        hand_over,
        in_specs=[vmem, vmem],
        out_specs=[hbm, hbm],
        out_shape=[
            jax.ShapeDtypeStruct(gradient.shape, F32),
            jax.ShapeDtypeStruct(residual.shape, F32),
        ],
        scratch_shapes=[sem((2,))],
        name="hand_over",
    )(gradient, residual)
    return gradient.reshape(points // 2), residual


def ring_on_device(reflectivity, source_green, receiver_green, observed, source_table, receiver_table):
    freqs, points, comps, width = source_green.shape
    per = observed.shape[1]
    lanes = observed.shape[3]
    n = lax.axis_size("slab")
    pairs = SIDE * SIDE
    wide = comps * width
    tall = TILE * wide // lanes
    rows = points // lanes
    vmem = pl.BlockSpec(memory_space=pltpu.VMEM)
    smem = pl.BlockSpec(memory_space=pltpu.SMEM)
    hbm = pl.BlockSpec(memory_space=pl.ANY)
    hop_sems = pltpu.SemaphoreType.DMA((freqs, 2, 2, n // 2))
    gradient, residual = pl.pallas_call(
        functools.partial(ring_kernel, n, n == 8),
        in_specs=[smem, smem, vmem, hbm, hbm, vmem],
        out_specs=[vmem, vmem],
        out_shape=[
            jax.ShapeDtypeStruct((rows // 2, lanes), F32),
            jax.ShapeDtypeStruct(observed.shape, F32),
        ],
        scratch_shapes=[
            pltpu.VMEM((2, 2, tall, lanes), BF16),
            pltpu.VMEM((tall, lanes), F32),
            pltpu.VMEM((tall, lanes), F32),
            pltpu.VMEM((freqs, points, wide), BF16),
            pltpu.VMEM((freqs, points, wide), BF16),
            pltpu.VMEM((TILE, wide), BF16),
            pltpu.VMEM((wide, wide), F32),
            pltpu.VMEM((freqs, pairs + 1, 2, lanes, lanes), F32),
            pltpu.VMEM((freqs, 2, 2, per, lanes, lanes), F32),
            pltpu.VMEM((freqs, 2, 2, n // 2, per, lanes, lanes), F32),
            pltpu.VMEM((n * per, lanes, lanes), BF16),
            pltpu.VMEM((n * per, lanes, lanes), BF16),
            pltpu.VMEM((n * per, lanes, lanes), BF16),
            pltpu.VMEM((n * per, lanes, lanes), BF16),
            pltpu.VMEM((freqs, 2, width, width), BF16),
            pltpu.VMEM((points, lanes), F32),
            pltpu.VMEM((rows, lanes), F32),
            pltpu.VMEM((rows // 2, lanes), F32),
            pltpu.SemaphoreType.DMA((2, 2)),
            hop_sems,
            hop_sems,
            hop_sems,
            hop_sems,
            pltpu.SemaphoreType.DMA,
            pltpu.SemaphoreType.DMA,
        ],
        compiler_params=pltpu.CompilerParams(collective_id=0, has_side_effects=True, vmem_limit_bytes=VMEM_BYTES),
        name="migration",
    )(
        source_table,
        receiver_table,
        reflectivity.reshape(rows, lanes),
        interleaved_tiles(source_green, lanes),
        interleaved_tiles(receiver_green, lanes),
        observed,
    )
    return gradient.reshape(points // 2), residual


def solution(mesh):
    on_device = grid_on_device if mesh.shape["slab"] == SLICES else ring_on_device
    return jax.shard_map(
        on_device,
        mesh=mesh,
        in_specs=(
            P(("parts", "slab")),
            P("freq", ("parts", "slab"), None, None),
            P("freq", ("parts", "slab"), None, None),
            P("freq", ("parts", "slab"), None, None, None),
            P(("parts", "slab"), None),
            P(("parts", "slab"), None),
        ),
        out_specs=(P(("parts", "slab", "freq")), P("freq", ("parts", "slab"), None, None, None)),
        check_vma=False,
    )
```

```python
import functools

import jax
import jax.numpy as jnp
from jax import lax
from jax.experimental import pallas as pl
from jax.experimental.pallas import tpu as pltpu
from jax.sharding import PartitionSpec as P

RB = 4
TILE = 1024
SPAN = 2048
SIDE = 2
MESH = pl.DeviceIdType.MESH
F32 = jnp.float32
BF16 = jnp.bfloat16
I16 = jnp.int16
STRIP = 16
SLICES = 8
REACH = 32600.0
VMEM_BYTES = 56 * 2**20


def hand_over(grad_in, res_in, grad_out, res_out, sems):
    copies = [
        pltpu.make_async_copy(grad_in, grad_out, sems.at[0]),
        pltpu.make_async_copy(res_in, res_out, sems.at[1]),
    ]
    for copy in copies:
        copy.start()
    for copy in copies:
        copy.wait()


def unit_of(values):
    peak = functools.reduce(
        jnp.maximum, [jnp.max(jnp.abs(value), axis=0, keepdims=True) for value in values]
    )
    return jnp.maximum(peak, 1e-30) * (1.0 / REACH)


def grid_kernel(plan, st_hbm, rt_hbm, refl_ref, g_hbm, r_hbm, obs_ref, grad_hbm, res_hbm,
                st_ref, rt_ref, grad_ref, res_ref, out_sem, obs, refl_own, raw, g32, r32, gd, rd, scaled_a, acc, part, adj, total, summed, other,
                tab_send, tab_recv, tab, unit_send, unit_recv, obs_send, obs_recv, obs_all, sum_send, sum_recv,
                terms, res_all, rounded, use_send, ret_send, ret_recv,
                in_sem, raw_sem, unit_ss, unit_rs, tab_ss, tab_rs, tab_local, obs_ss, obs_rs, sum_ss, sum_rs, use_ss, use_rs,
                ret_ss, ret_rs, ex_send, ex_recv):
    per = obs.shape[1]
    lanes = obs.shape[3]
    freqs, points, wide = gd.shape
    half = wide // 2
    tiles = points // TILE
    groups = TILE // lanes
    pairs = SIDE * SIDE
    n = lanes // STRIP
    panels = n * per
    me = lax.axis_index("slab")
    mine_f = lax.axis_index("freq")
    order = sorted(range(1, n), key=lambda d: abs(d - n // 2))

    def to(d):
        return lax.rem(me + d, n)

    def source(d):
        return lax.rem(me + n - d, n)

    def strip(at):
        return pl.ds(pl.multiple_of(at * STRIP, STRIP), STRIP)

    barrier = pltpu.get_barrier_semaphore()
    for d in range(n - 1, 0, -1):
        pl.semaphore_signal(barrier, inc=1, device_id={"slab": me ^ d}, device_id_type=MESH)
    pl.semaphore_signal(barrier, inc=1, device_id={"freq": 1 - mine_f}, device_id_type=MESH)

    def fetches(q, slot):
        return (
            pltpu.make_async_copy(g_hbm.at[q], raw.at[slot, 0], raw_sem.at[slot, 0]),
            pltpu.make_async_copy(r_hbm.at[q], raw.at[slot, 1], raw_sem.at[slot, 1]),
        )

    obs_load = pltpu.make_async_copy(obs_ref, obs, in_sem.at[0])
    refl_load = pltpu.make_async_copy(refl_ref, refl_own, in_sem.at[1])
    tab_loads = (
        pltpu.make_async_copy(st_hbm, st_ref, in_sem.at[2]),
        pltpu.make_async_copy(rt_hbm, rt_ref, in_sem.at[3]),
    )
    for copy in tab_loads:
        copy.start()
    obs_load.start()
    refl_load.start()
    for q in range(2):
        for copy in fetches(q, q):
            copy.start()

    terms[:, pairs] = jnp.zeros((n, STRIP, lanes), F32)

    def shape_tile(q):
        f, t = q // tiles, q % tiles
        slot = q % 2
        for copy in fetches(q, slot):
            copy.wait()
        g32[...] = raw[slot, 0].astype(F32)
        r32[...] = raw[slot, 1].astype(F32)

        @pl.when(q + 2 < freqs * tiles)
        def _():
            for copy in fetches(q + 2, slot):
                copy.start()

        refl = refl_own[pl.ds(pl.multiple_of(t * groups, groups), groups), :]
        weight = jnp.concatenate(
            [jnp.broadcast_to(refl[b : b + 1, :], (lanes, lanes)).T for b in range(groups)], axis=0
        )
        here = pl.ds(pl.multiple_of(t * TILE, TILE), TILE)
        for block in range(SIDE):
            for comp in range(2):
                lines = pl.ds(block * 2 + comp, TILE, stride=2 * SIDE)
                cols = slice(comp * half + block * lanes, comp * half + (block + 1) * lanes)
                green = g32[lines, :]
                gd[f, here, cols] = green.astype(BF16)
                scaled_a[:, cols] = (green * weight).astype(BF16)
                rd[f, here, cols] = r32[lines, :].astype(BF16)

    def sum_tile(q):
        f, t = q // tiles, q % tiles
        here = pl.ds(pl.multiple_of(t * TILE, TILE), TILE)
        acc[...] += lax.dot_general(
            scaled_a[...], rd[f, here, :], (((0,), (0,)), ((), ())), preferred_element_type=F32
        )

    def forward(start, stop):
        def body(q, carry):
            shape_tile(q)
            sum_tile(q)
            return carry

        lax.fori_loop(start, stop, body, 0)

    def clear():
        acc[...] = jnp.zeros_like(acc)

    def squares(i, j):
        s_re = slice(i * lanes, (i + 1) * lanes)
        s_im = slice(half + i * lanes, half + (i + 1) * lanes)
        r_re = slice(j * lanes, (j + 1) * lanes)
        r_im = slice(half + j * lanes, half + (j + 1) * lanes)
        return s_re, s_im, r_re, r_im

    def finish_part(f):
        for k in range(pairs):
            s_re, s_im, r_re, r_im = squares(k // SIDE, k % SIDE)
            part[f, k, 0] = acc[s_re, r_re] - acc[s_im, r_im]
            part[f, k, 1] = acc[s_re, r_im] + acc[s_im, r_re]

    def remote(src, dst, send, recv, d):
        return pltpu.make_async_remote_copy(
            src_ref=src, dst_ref=dst, send_sem=send, recv_sem=recv,
            device_id={"slab": to(d)}, device_id_type=MESH,
        )

    def tab_copy(d, at):
        return remote(tab_send, tab_recv.at[at], tab_ss.at[d], tab_rs.at[d], d)

    def unit_copy(kind, d, at):
        return remote(
            unit_send.at[kind], unit_recv.at[kind, at], unit_ss.at[kind, d], unit_rs.at[kind, d], d
        )

    def obs_copy(d, at):
        return remote(obs_send.at[to(d)], obs_recv.at[at], obs_ss.at[d], obs_rs.at[d], d)

    def sum_copy(f, c, d, at):
        part_of = pl.ds(c * pairs, pairs)
        return remote(
            sum_send.at[f, to(d), part_of], sum_recv.at[f, at, part_of],
            sum_ss.at[f, c, d], sum_rs.at[f, c, d], d,
        )

    def use_copy(f, c, d, at):
        return remote(
            use_send.at[f, c, to(d)], adj.at[f, c, :, strip(at), :],
            use_ss.at[f, c, d], use_rs.at[f, c, d], d,
        )

    def ret_copy(d, at):
        return remote(ret_send.at[to(d)], ret_recv.at[at], ret_ss.at[d], ret_rs.at[d], d)

    def encode(kind, values, out):
        unit = unit_of(values)
        unit_send[kind] = unit
        gain = 1.0 / unit
        for at, value in enumerate(values):
            code = jnp.round(value * gain).astype(I16)
            out[:, at] = code.reshape(n, STRIP, lanes)

    fcks = [(f, c, k) for f in range(freqs) for c in range(2) for k in range(per)]

    def greet():
        for copy in tab_loads:
            copy.wait()
        lane = lax.broadcasted_iota(jnp.int32, tab_send.shape, 1)
        line = jnp.zeros(tab_send.shape, jnp.int32)
        for at, value in enumerate((st_ref[0, 0], st_ref[0, 1], rt_ref[0, 0], rt_ref[0, 1])):
            line = jnp.where(lane == at, value, line)
        tab_send[...] = line
        tab_recv[me] = line
        obs_load.wait()
        refl_load.wait()
        encode(freqs, [obs[f, k, c] for f, c, k in fcks], obs_send)
        pl.semaphore_wait(barrier, n)
        for d in order:
            tab_copy(d, me).start()
            unit_copy(freqs, d, me).start()
            obs_copy(d, me).start()

    def take_tables():
        for d in order:
            tab_copy(d, source(d)).wait_recv()
        copy = pltpu.make_async_copy(tab_recv, tab, tab_local)
        copy.start()
        copy.wait()

    def take_obs():
        for d in order:
            at = source(d)
            unit_copy(freqs, d, at).wait_recv()
            obs_copy(d, at).wait_recv()
            unit = unit_recv[freqs, at]
            for block, (f, c, k) in enumerate(fcks):
                obs_all[f, c, at * per + k] = obs_recv[at, block].astype(F32) * unit
        for f, c, k in fcks:
            obs_all[f, c, me * per + k] = obs[f, k, c, strip(me), :]

    def share(f):
        encode(f, [part[f, b, c] for c in range(2) for b in range(pairs)], sum_send.at[f])
        for d in order:
            unit_copy(f, d, me).start()
            sum_copy(f, 0, d, me).start()
        for d in order:
            sum_copy(f, 1, d, me).start()

    def tables():
        return [tuple(tab[s, 0, at] for at in range(4)) for s in range(n)]

    def reduce(f, c):
        for b in range(pairs):
            terms[me, b] = part[f, b, c, strip(me), :]
        for d in order:
            at = source(d)
            if c == 0:
                unit_copy(f, d, at).wait_recv()
            sum_copy(f, c, d, at).wait_recv()
            unit = unit_recv[f, at]
            for b in range(pairs):
                terms[at, b] = sum_recv[f, at, c * pairs + b].astype(F32) * unit
        rows_of, cols_of = [], []
        for table in tables():
            rows_of.append([
                jnp.where(table[0] == sb, 0, jnp.where(table[1] == sb, SIDE, pairs))
                for sb in range(panels // RB)
            ])
            cols_of.append([
                jnp.where(table[2] == rb, 0, jnp.where(table[3] == rb, 1, pairs)) for rb in range(RB)
            ])
        for panel in range(panels):
            value = -obs_all[f, c, panel]
            for s in range(n):
                index = jnp.minimum(rows_of[s][panel // RB] + cols_of[s][panel % RB], pairs)
                value = value + terms[s, index]
            res_all[f, c, panel] = value
            rounded[panel] = value.astype(BF16)
        for at, table in enumerate(tables()):
            for b in range(pairs):
                use_send[f, c, at, b] = rounded[table[b // SIDE] * RB + table[2 + b % SIDE]]
        for d in order:
            use_copy(f, c, d, me).start()
        for b in range(pairs):
            adj[f, c, b, strip(me), :] = use_send[f, c, me, b]

    def give_back():
        unit = unit_of([res_all[f, c, p] for f in range(freqs) for c in range(2) for p in range(panels)])
        unit_send[freqs + 1] = unit
        gain = 1.0 / unit
        for at in range(n):
            for block, (f, c, k) in enumerate(fcks):
                ret_send[at, block] = jnp.round(res_all[f, c, at * per + k] * gain).astype(I16)
        for d in order:
            unit_copy(freqs + 1, d, me).start()
            ret_copy(d, me).start()

    def take_back():
        for f, c, k in fcks:
            res_ref[f, k, c, strip(me), :] = res_all[f, c, me * per + k]
        for d in order:
            at = source(d)
            unit_copy(freqs + 1, d, at).wait_recv()
            ret_copy(d, at).wait_recv()
            unit = unit_recv[freqs + 1, at]
            for block, (f, c, k) in enumerate(fcks):
                res_ref[f, k, c, strip(at), :] = ret_recv[at, block].astype(F32) * unit

    def take_use(f, c):
        for d in order:
            use_copy(f, c, d, source(d)).wait_recv()

    def adjoint_terms(f, c, t):
        here = pl.ds(pl.multiple_of(t * SPAN, SPAN), SPAN)
        data = jnp.concatenate(
            [
                jnp.concatenate([adj[f, c, i * SIDE + j] for j in range(SIDE)], axis=1)
                for i in range(SIDE)
            ],
            axis=0,
        )
        by_re = jnp.dot(gd[f, here, :half], data, preferred_element_type=F32)
        by_im = jnp.dot(gd[f, here, half:], data, preferred_element_type=F32)
        rec_re = rd[f, here, :half].astype(F32)
        rec_im = rd[f, here, half:].astype(F32)
        if c == 0:
            terms = rec_re * by_re - rec_im * by_im
        else:
            terms = rec_re * by_im + rec_im * by_re
        result = terms[:, :lanes]
        for at in range(lanes, half, lanes):
            result = result + terms[:, at : at + lanes]
        return here, result

    def adjoint(f, c, turn):
        def body(t, carry):
            here, result = adjoint_terms(f, c, t)
            if turn > 0:
                result = total[here, :] + result
            if turn < 2 * freqs - 1:
                total[here, :] = result
                return carry
            sums = [
                jnp.sum(result[b * lanes : (b + 1) * lanes, :].T, axis=0, keepdims=True)
                for b in range(SPAN // lanes)
            ]
            summed[pl.ds(pl.multiple_of(t * SPAN // lanes, SPAN // lanes), SPAN // lanes), :] = jnp.concatenate(sums, 0)
            return carry

        lax.fori_loop(0, points // SPAN, body, 0)

    steps = {
        "greet": greet, "tables": take_tables, "take_obs": take_obs,
        "shape": shape_tile, "sum": sum_tile, "forward": forward, "clear": clear, "part": finish_part, "share": share, "reduce": reduce, "back": give_back,
        "use": take_use, "adjoint": adjoint,
    }
    for name, *rest in plan(tiles):
        steps[name](*rest)

    own_rows = grad_ref.shape[0]
    swap = pltpu.make_async_remote_copy(
        src_ref=summed.at[pl.ds(pl.multiple_of((1 - mine_f) * own_rows, own_rows), own_rows)],
        dst_ref=other,
        send_sem=ex_send,
        recv_sem=ex_recv,
        device_id={"freq": 1 - mine_f},
        device_id_type=MESH,
    )
    swap.start()

    take_back()
    res_store = pltpu.make_async_copy(res_ref, res_hbm, out_sem.at[0])
    res_store.start()
    for d in order:
        tab_copy(d, me).wait_send()
        obs_copy(d, me).wait_send()
        ret_copy(d, me).wait_send()
        for kind in range(freqs + 2):
            unit_copy(kind, d, me).wait_send()
        for f in range(freqs):
            for c in range(2):
                sum_copy(f, c, d, me).wait_send()
                use_copy(f, c, d, me).wait_send()
    swap.wait()
    mine = summed[pl.ds(pl.multiple_of(mine_f * own_rows, own_rows), own_rows), :]
    grad_ref[...] = mine + other[...]
    grad_store = pltpu.make_async_copy(grad_ref, grad_hbm, out_sem.at[1])
    grad_store.start()
    grad_store.wait()
    res_store.wait()


def grid_plan(tiles):
    plan = [("greet",), ("clear",), ("forward", 0, tiles), ("part", 0), ("share", 0), ("clear",)]
    plan += [("forward", tiles, 2 * tiles), ("part", 1), ("share", 1), ("tables",), ("take_obs",)]
    plan += [
        ("reduce", 0, 0),
        ("reduce", 0, 1),
        ("reduce", 1, 0),
        ("use", 0, 0),
        ("adjoint", 0, 0, 0),
        ("reduce", 1, 1),
        ("back",),
        ("use", 0, 1),
        ("adjoint", 0, 1, 1),
        ("use", 1, 0),
        ("adjoint", 1, 0, 2),
        ("use", 1, 1),
        ("adjoint", 1, 1, 3),
    ]
    return plan


def ring_kernel(n, snake, st_ref, rt_ref, refl_ref, g_hbm, r_hbm, obs_ref, grad_ref, res_ref,
           raw, g32, r32, gd, rd, scaled, acc, part, first, held, gath_a, gath_b, gath_c, gath_d, adj, total, summed, other,
           raw_sem, rs_send, rs_recv, ag_send, ag_recv, ex_send, ex_recv):
    per = obs_ref.shape[1]
    lanes = obs_ref.shape[3]
    freqs, points, wide = gd.shape
    half = wide // 2
    tiles = points // TILE
    groups = TILE // lanes
    pairs = SIDE * SIDE
    gath = ((gath_a, gath_b), (gath_c, gath_d))
    me = lax.axis_index("slab")
    mine_f = lax.axis_index("freq")

    def index_of(pos):
        if not snake:
            return pos
        return 2 * pos + (pos // (n // 2)) * (2 * n - 1 - 4 * pos)

    place = me // 2 + (me % 2) * (n - 1 - 2 * (me // 2)) if snake else me
    ways = (1, -1)
    targets = tuple(index_of((place + way + n) % n) for way in ways)
    low = (n - 1) // 2
    high = n - 1 - low

    barrier = pltpu.get_barrier_semaphore()
    for target in targets:
        pl.semaphore_signal(barrier, inc=1, device_id={"slab": target}, device_id_type=MESH)
    pl.semaphore_signal(barrier, inc=1, device_id={"freq": 1 - mine_f}, device_id_type=MESH)

    def fetches(q, slot):
        return (
            pltpu.make_async_copy(g_hbm.at[q], raw.at[slot, 0], raw_sem.at[slot, 0]),
            pltpu.make_async_copy(r_hbm.at[q], raw.at[slot, 1], raw_sem.at[slot, 1]),
        )

    for q in range(2):
        for copy in fetches(q, q):
            copy.start()

    def forward_tile(f, t):
        q = f * tiles + t
        slot = q % 2
        for copy in fetches(q, slot):
            copy.wait()
        g32[...] = raw[slot, 0].astype(F32)
        r32[...] = raw[slot, 1].astype(F32)

        @pl.when(q + 2 < freqs * tiles)
        def _():
            for copy in fetches(q + 2, slot):
                copy.start()

        refl = refl_ref[pl.ds(pl.multiple_of(t * groups, groups), groups), :]
        weight = jnp.concatenate(
            [jnp.broadcast_to(refl[b : b + 1, :], (lanes, lanes)).T for b in range(groups)], axis=0
        )
        here = pl.ds(pl.multiple_of(t * TILE, TILE), TILE)
        for block in range(SIDE):
            for comp in range(2):
                rows = pl.ds(block * 2 + comp, TILE, stride=2 * SIDE)
                cols = slice(comp * half + block * lanes, comp * half + (block + 1) * lanes)
                green = g32[rows, :]
                gd[f, here, cols] = green.astype(BF16)
                scaled[:, cols] = (green * weight).astype(BF16)
                rd[f, here, cols] = r32[rows, :].astype(BF16)
        prod = lax.dot_general(
            scaled[...], rd[f, here, :], (((0,), (0,)), ((), ())), preferred_element_type=F32
        )
        acc[...] += prod

    def forward(f, start, stop):
        def body(t, carry):
            forward_tile(f, t)
            return carry

        lax.fori_loop(start, stop, body, 0)

    def squares(i, j):
        s_re = slice(i * lanes, (i + 1) * lanes)
        s_im = slice(half + i * lanes, half + (i + 1) * lanes)
        r_re = slice(j * lanes, (j + 1) * lanes)
        r_im = slice(half + j * lanes, half + (j + 1) * lanes)
        return s_re, s_im, r_re, r_im

    def finish_part(f):
        for k in range(pairs):
            s_re, s_im, r_re, r_im = squares(k // SIDE, k % SIDE)
            part[f, k, 0] = acc[s_re, r_re] - acc[s_im, r_im]
            part[f, k, 1] = acc[s_re, r_im] + acc[s_im, r_re]
        part[f, pairs] = jnp.zeros((2, lanes, lanes), F32)

    def hops(f, w):
        return high if f == w else low

    lanes_of = [(c, w) for c in range(2) for w in range(2)]

    def held_at(panel):
        sb = panel // RB
        rb = panel % RB
        i = jnp.where(st_ref[0, 0] == sb, 0, jnp.where(st_ref[0, 1] == sb, SIDE, 2 * pairs))
        j = jnp.where(rt_ref[0, 0] == rb, 0, jnp.where(rt_ref[0, 1] == rb, 1, 2 * pairs))
        return jnp.minimum(i + j, pairs)

    def own(f, c, w, away):
        owner = index_of((place + ways[w] * away + n) % n)
        return [part[f, held_at(owner * per + k), c] for k in range(per)]

    def rs_copy(f, c, w, src, step):
        return pltpu.make_async_remote_copy(
            src_ref=src,
            dst_ref=held.at[f, c, w, step],
            send_sem=rs_send.at[f, c, w, step],
            recv_sem=rs_recv.at[f, c, w, step],
            device_id={"slab": targets[w]},
            device_id_type=MESH,
        )

    def ag_copy(f, c, w, step, away):
        owner = index_of((place - ways[w] * away + n) % n)
        view = gath[f][c].at[pl.ds(owner * per, per)]
        return pltpu.make_async_remote_copy(
            src_ref=view,
            dst_ref=view,
            send_sem=ag_send.at[f, c, w, step],
            recv_sem=ag_recv.at[f, c, w, step],
            device_id={"slab": targets[w]},
            device_id_type=MESH,
        )

    def rs_start(f):
        for c, w in lanes_of:
            mine = own(f, c, w, hops(f, w))
            for k in range(per):
                first[f, c, w, k] = mine[k]
            rs_copy(f, c, w, first.at[f, c, w], 0).start()

    def rs_pass(f, step, only=None):
        for c, w in lanes_of:
            if only is not None and w != only:
                continue
            rs_copy(f, c, w, held.at[f, c, w, step], step).wait_recv()
            mine = own(f, c, w, hops(f, w) - step - 1)
            for k in range(per):
                held[f, c, w, step, k] = held[f, c, w, step, k] + mine[k]
            rs_copy(f, c, w, held.at[f, c, w, step], step + 1).start()

    def ag_pass(f, step, only=None):
        for c, w in lanes_of:
            if only is not None and w != only:
                continue
            ag_copy(f, c, w, step, step + 1).wait_recv()
            ag_copy(f, c, w, step + 1, step + 1).start()

    def rs_longer(f):
        if high > low:
            rs_pass(f, high - 2, f)

    def ag_longer(f):
        if high > low:
            ag_pass(f, high - 2, f)

    def rs_finish(f):
        for c in range(2):
            for w in range(2):
                last = hops(f, w) - 1
                rs_copy(f, c, w, held.at[f, c, w, last], last).wait_recv()
            mine = own(f, c, 0, 0)
            for k in range(per):
                value = (
                    held[f, c, 0, hops(f, 0) - 1, k] + held[f, c, 1, hops(f, 1) - 1, k] + mine[k]
                ) - obs_ref[f, k, c]
                res_ref[f, k, c] = value
                gath[f][c][me * per + k] = value.astype(BF16)
            for w in range(2):
                ag_copy(f, c, w, 0, 0).start()

    def ag_finish(f, c):
        for w in range(2):
            last = hops(f, w) - 1
            ag_copy(f, c, w, last, last + 1).wait_recv()
        for k in range(pairs):
            i, j = k // SIDE, k % SIDE
            panel = st_ref[0, i] * RB + rt_ref[0, j]
            s_re, s_im, r_re, r_im = squares(i, j)
            adj[f, c, s_re, r_re] = gath[f][c][panel]

    def adjoint_terms(f, c, t):
        here = pl.ds(pl.multiple_of(t * TILE, TILE), TILE)
        data = adj[f, c]
        by_re = jnp.dot(gd[f, here, :half], data, preferred_element_type=F32)
        by_im = jnp.dot(gd[f, here, half:], data, preferred_element_type=F32)
        rec_re = rd[f, here, :half].astype(F32)
        rec_im = rd[f, here, half:].astype(F32)
        if c == 0:
            terms = rec_re * by_re - rec_im * by_im
        else:
            terms = rec_re * by_im + rec_im * by_re
        result = terms[:, :lanes]
        for at in range(lanes, half, lanes):
            result = result + terms[:, at : at + lanes]
        return here, result

    def adjoint(f, c):
        def body(t, carry):
            here, result = adjoint_terms(f, c, t)
            if f + c > 0:
                result = total[here, :] + result
            if f + c < 2:
                total[here, :] = result
                return carry
            rows = [
                jnp.sum(result[b * lanes : (b + 1) * lanes, :].T, axis=0, keepdims=True)
                for b in range(groups)
            ]
            summed[pl.ds(pl.multiple_of(t * groups, groups), groups), :] = jnp.concatenate(rows, 0)
            return carry

        lax.fori_loop(0, tiles, body, 0)

    acc[...] = jnp.zeros_like(acc)
    forward(0, 0, tiles)
    finish_part(0)
    pl.semaphore_wait(barrier, 3)
    rs_start(0)
    acc[...] = jnp.zeros_like(acc)
    forward(1, 0, tiles // 2)
    rs_pass(0, 0)
    forward(1, tiles // 2, tiles)
    finish_part(1)
    rs_start(1)

    def rs_both(step, carry):
        rs_pass(0, step)
        rs_pass(1, step - 1)
        return carry

    lax.fori_loop(1, low - 1, rs_both, 0)
    rs_longer(0)
    rs_pass(1, low - 2)
    rs_finish(0)
    rs_longer(1)
    ag_pass(0, 0)
    rs_finish(1)

    def ag_both(step, carry):
        ag_pass(0, step)
        ag_pass(1, step - 1)
        return carry

    lax.fori_loop(1, low - 1, ag_both, 0)
    ag_longer(0)
    ag_pass(1, low - 2)
    ag_finish(0, 0)
    adjoint(0, 0)
    ag_longer(1)
    ag_finish(0, 1)
    adjoint(0, 1)
    ag_finish(1, 0)
    adjoint(1, 0)
    ag_finish(1, 1)
    adjoint(1, 1)

    own_rows = grad_ref.shape[0]
    swap = pltpu.make_async_remote_copy(
        src_ref=summed.at[pl.ds(pl.multiple_of((1 - mine_f) * own_rows, own_rows), own_rows)],
        dst_ref=other,
        send_sem=ex_send,
        recv_sem=ex_recv,
        device_id={"freq": 1 - mine_f},
        device_id_type=MESH,
    )
    swap.start()

    def drain(step, carry):
        for f in range(2):
            for c, w in lanes_of:
                rs_copy(f, c, w, first.at[f, c, w], step).wait_send()
                ag_copy(f, c, w, step, step).wait_send()
        return carry

    lax.fori_loop(0, low, drain, 0)
    if high > low:
        for f in range(2):
            for c in range(2):
                rs_copy(f, c, f, first.at[f, c, f], high - 1).wait_send()
                ag_copy(f, c, f, high - 1, high - 1).wait_send()
    swap.wait()
    mine = summed[pl.ds(pl.multiple_of(mine_f * own_rows, own_rows), own_rows), :]
    grad_ref[...] = mine + other[...]


def interleaved_tiles(green, lanes):
    freqs, points, comps, width = green.shape
    view = green.reshape(freqs, points, comps, width // lanes, lanes).transpose(0, 1, 3, 2, 4)
    tiles = freqs * points // TILE
    return view.reshape(tiles, TILE * comps * width // lanes, lanes)


def grid_on_device(reflectivity, source_green, receiver_green, observed, source_table, receiver_table):
    freqs, points, comps, width = source_green.shape
    per = observed.shape[1]
    lanes = observed.shape[3]
    pairs = SIDE * SIDE
    n = lanes // STRIP
    panels = n * per
    blocks = 2 * pairs
    wide = comps * width
    tall = TILE * wide // lanes
    lines = points // lanes
    vmem = pl.BlockSpec(memory_space=pltpu.VMEM)
    smem = pl.BlockSpec(memory_space=pltpu.SMEM)
    hbm = pl.BlockSpec(memory_space=pl.ANY)
    sem = pltpu.SemaphoreType.DMA

    def codes(*shape):
        return pltpu.VMEM(shape + (STRIP, lanes), I16)

    gradient, residual = pl.pallas_call(
        functools.partial(grid_kernel, grid_plan),
        in_specs=[hbm, hbm, hbm, hbm, hbm, hbm],
        out_specs=[hbm, hbm],
        out_shape=[
            jax.ShapeDtypeStruct((lines // 2, lanes), F32),
            jax.ShapeDtypeStruct(observed.shape, F32),
        ],
        scratch_shapes=[
            pltpu.SMEM(source_table.shape, jnp.int32),
            pltpu.SMEM(receiver_table.shape, jnp.int32),
            pltpu.VMEM((lines // 2, lanes), F32),
            pltpu.VMEM(observed.shape, F32),
            sem((2,)),
            pltpu.VMEM(observed.shape, F32),
            pltpu.VMEM((lines, lanes), F32),
            pltpu.VMEM((2, 2, tall, lanes), BF16),
            pltpu.VMEM((tall, lanes), F32),
            pltpu.VMEM((tall, lanes), F32),
            pltpu.VMEM((freqs, points, wide), BF16),
            pltpu.VMEM((freqs, points, wide), BF16),
            pltpu.VMEM((TILE, wide), BF16),
            pltpu.VMEM((wide, wide), F32),
            pltpu.VMEM((freqs, pairs, 2, lanes, lanes), F32),
            pltpu.VMEM((freqs, 2, pairs, lanes, lanes), BF16),
            pltpu.VMEM((points, lanes), F32),
            pltpu.VMEM((lines, lanes), F32),
            pltpu.VMEM((lines // 2, lanes), F32),
            pltpu.VMEM((8, 128), jnp.int32),
            pltpu.VMEM((n, 8, 128), jnp.int32),
            pltpu.SMEM((n, 8, 128), jnp.int32),
            pltpu.VMEM((freqs + 2, 1, lanes), F32),
            pltpu.VMEM((freqs + 2, n, 1, lanes), F32),
            codes(n, blocks), codes(n, blocks),
            pltpu.VMEM((freqs, 2, panels, STRIP, lanes), F32),
            codes(freqs, n, blocks), codes(freqs, n, blocks),
            pltpu.VMEM((n, pairs + 1, STRIP, lanes), F32),
            pltpu.VMEM((freqs, 2, panels, STRIP, lanes), F32),
            pltpu.VMEM((panels, STRIP, lanes), BF16),
            pltpu.VMEM((freqs, 2, n, pairs, STRIP, lanes), BF16),
            codes(n, blocks), codes(n, blocks),
            sem((4,)),
            sem((2, 2)),
            sem((freqs + 2, n)), sem((freqs + 2, n)),
            sem((n,)), sem((n,)), sem,
            sem((n,)), sem((n,)),
            sem((freqs, 2, n)), sem((freqs, 2, n)),
            sem((freqs, 2, n)), sem((freqs, 2, n)),
            sem((n,)), sem((n,)),
            sem, sem,
        ],
        compiler_params=pltpu.CompilerParams(
            collective_id=0, has_side_effects=True, vmem_limit_bytes=VMEM_BYTES
        ),
        name="migration",
    )(
        source_table,
        receiver_table,
        reflectivity.reshape(lines, lanes),
        interleaved_tiles(source_green, lanes),
        interleaved_tiles(receiver_green, lanes),
        observed,
    )
    gradient, residual = pl.pallas_call(
        hand_over,
        in_specs=[vmem, vmem],
        out_specs=[hbm, hbm],
        out_shape=[
            jax.ShapeDtypeStruct(gradient.shape, F32),
            jax.ShapeDtypeStruct(residual.shape, F32),
        ],
        scratch_shapes=[sem((2,))],
        name="hand_over",
    )(gradient, residual)
    return gradient.reshape(points // 2), residual


def ring_on_device(reflectivity, source_green, receiver_green, observed, source_table, receiver_table):
    freqs, points, comps, width = source_green.shape
    per = observed.shape[1]
    lanes = observed.shape[3]
    n = lax.axis_size("slab")
    pairs = SIDE * SIDE
    wide = comps * width
    tall = TILE * wide // lanes
    rows = points // lanes
    vmem = pl.BlockSpec(memory_space=pltpu.VMEM)
    smem = pl.BlockSpec(memory_space=pltpu.SMEM)
    hbm = pl.BlockSpec(memory_space=pl.ANY)
    hop_sems = pltpu.SemaphoreType.DMA((freqs, 2, 2, n // 2))
    gradient, residual = pl.pallas_call(
        functools.partial(ring_kernel, n, n == 8),
        in_specs=[smem, smem, vmem, hbm, hbm, vmem],
        out_specs=[vmem, vmem],
        out_shape=[
            jax.ShapeDtypeStruct((rows // 2, lanes), F32),
            jax.ShapeDtypeStruct(observed.shape, F32),
        ],
        scratch_shapes=[
            pltpu.VMEM((2, 2, tall, lanes), BF16),
            pltpu.VMEM((tall, lanes), F32),
            pltpu.VMEM((tall, lanes), F32),
            pltpu.VMEM((freqs, points, wide), BF16),
            pltpu.VMEM((freqs, points, wide), BF16),
            pltpu.VMEM((TILE, wide), BF16),
            pltpu.VMEM((wide, wide), F32),
            pltpu.VMEM((freqs, pairs + 1, 2, lanes, lanes), F32),
            pltpu.VMEM((freqs, 2, 2, per, lanes, lanes), F32),
            pltpu.VMEM((freqs, 2, 2, n // 2, per, lanes, lanes), F32),
            pltpu.VMEM((n * per, lanes, lanes), BF16),
            pltpu.VMEM((n * per, lanes, lanes), BF16),
            pltpu.VMEM((n * per, lanes, lanes), BF16),
            pltpu.VMEM((n * per, lanes, lanes), BF16),
            pltpu.VMEM((freqs, 2, width, width), BF16),
            pltpu.VMEM((points, lanes), F32),
            pltpu.VMEM((rows, lanes), F32),
            pltpu.VMEM((rows // 2, lanes), F32),
            pltpu.SemaphoreType.DMA((2, 2)),
            hop_sems,
            hop_sems,
            hop_sems,
            hop_sems,
            pltpu.SemaphoreType.DMA,
            pltpu.SemaphoreType.DMA,
        ],
        compiler_params=pltpu.CompilerParams(collective_id=0, has_side_effects=True, vmem_limit_bytes=VMEM_BYTES),
        name="migration",
    )(
        source_table,
        receiver_table,
        reflectivity.reshape(rows, lanes),
        interleaved_tiles(source_green, lanes),
        interleaved_tiles(receiver_green, lanes),
        observed,
    )
    return gradient.reshape(points // 2), residual


def solution(mesh):
    on_device = grid_on_device if mesh.shape["slab"] == SLICES else ring_on_device
    return jax.shard_map(
        on_device,
        mesh=mesh,
        in_specs=(
            P(("parts", "slab")),
            P("freq", ("parts", "slab"), None, None),
            P("freq", ("parts", "slab"), None, None),
            P("freq", ("parts", "slab"), None, None, None),
            P(("parts", "slab"), None),
            P(("parts", "slab"), None),
        ),
        out_specs=(P(("parts", "slab", "freq")), P("freq", ("parts", "slab"), None, None, None)),
        check_vma=False,
    )
```

```python
import functools

import jax
import jax.numpy as jnp
from jax import lax
from jax.experimental import pallas as pl
from jax.experimental.pallas import tpu as pltpu
from jax.sharding import PartitionSpec as P

RB = 4
TILE = 1024
SPAN = 2048
SIDE = 2
MESH = pl.DeviceIdType.MESH
F32 = jnp.float32
BF16 = jnp.bfloat16
I16 = jnp.int16
STRIP = 16
SLICES = 8
REACH = 32600.0
VMEM_BYTES = 56 * 2**20


def hand_over(grad_in, res_in, grad_out, res_out, sems):
    copies = [
        pltpu.make_async_copy(grad_in, grad_out, sems.at[0]),
        pltpu.make_async_copy(res_in, res_out, sems.at[1]),
    ]
    for copy in copies:
        copy.start()
    for copy in copies:
        copy.wait()


def unit_of(values):
    peak = functools.reduce(
        jnp.maximum, [jnp.max(jnp.abs(value), axis=0, keepdims=True) for value in values]
    )
    return jnp.maximum(peak, 1e-30) * (1.0 / REACH)


def grid_kernel(plan, st_hbm, rt_hbm, refl_ref, g_hbm, r_hbm, obs_ref, grad_hbm, res_hbm,
                st_ref, rt_ref, grad_ref, res_ref, out_sem, obs, refl_own, raw, g32, r32, gd, rd, scaled_a, acc, part, adj, total, summed, other,
                tab_send, tab_recv, tab, unit_send, unit_recv, obs_send, obs_recv, obs_all, sum_send, sum_recv,
                terms, res_all, rounded, use_send, ret_send, ret_recv,
                in_sem, raw_sem, unit_ss, unit_rs, tab_ss, tab_rs, tab_local, obs_ss, obs_rs, sum_ss, sum_rs, use_ss, use_rs,
                ret_ss, ret_rs, ex_send, ex_recv):
    per = obs.shape[1]
    lanes = obs.shape[3]
    freqs, points, wide = gd.shape
    half = wide // 2
    tiles = points // TILE
    groups = TILE // lanes
    pairs = SIDE * SIDE
    n = lanes // STRIP
    panels = n * per
    me = lax.axis_index("slab")
    mine_f = lax.axis_index("freq")
    order = sorted(range(1, n), key=lambda d: abs(d - n // 2))

    def to(d):
        return lax.rem(me + d, n)

    def source(d):
        return lax.rem(me + n - d, n)

    def strip(at):
        return pl.ds(pl.multiple_of(at * STRIP, STRIP), STRIP)

    barrier = pltpu.get_barrier_semaphore()
    for d in range(n - 1, 0, -1):
        pl.semaphore_signal(barrier, inc=1, device_id={"slab": me ^ d}, device_id_type=MESH)
    pl.semaphore_signal(barrier, inc=1, device_id={"freq": 1 - mine_f}, device_id_type=MESH)

    def fetches(q, slot):
        return (
            pltpu.make_async_copy(g_hbm.at[q], raw.at[slot, 0], raw_sem.at[slot, 0]),
            pltpu.make_async_copy(r_hbm.at[q], raw.at[slot, 1], raw_sem.at[slot, 1]),
        )

    obs_load = pltpu.make_async_copy(obs_ref, obs, in_sem.at[0])
    refl_load = pltpu.make_async_copy(refl_ref, refl_own, in_sem.at[1])
    tab_loads = (
        pltpu.make_async_copy(st_hbm, st_ref, in_sem.at[2]),
        pltpu.make_async_copy(rt_hbm, rt_ref, in_sem.at[3]),
    )
    for copy in tab_loads:
        copy.start()
    obs_load.start()
    refl_load.start()
    for q in range(2):
        for copy in fetches(q, q):
            copy.start()

    terms[:, pairs] = jnp.zeros((n, STRIP, lanes), F32)

    def shape_tile(q):
        f, t = q // tiles, q % tiles
        slot = q % 2
        for copy in fetches(q, slot):
            copy.wait()
        g32[...] = raw[slot, 0].astype(F32)
        r32[...] = raw[slot, 1].astype(F32)

        @pl.when(q + 2 < freqs * tiles)
        def _():
            for copy in fetches(q + 2, slot):
                copy.start()

        refl = refl_own[pl.ds(pl.multiple_of(t * groups, groups), groups), :]
        weight = jnp.concatenate(
            [jnp.broadcast_to(refl[b : b + 1, :], (lanes, lanes)).T for b in range(groups)], axis=0
        )
        here = pl.ds(pl.multiple_of(t * TILE, TILE), TILE)
        for block in range(SIDE):
            for comp in range(2):
                lines = pl.ds(block * 2 + comp, TILE, stride=2 * SIDE)
                cols = slice(comp * half + block * lanes, comp * half + (block + 1) * lanes)
                green = g32[lines, :]
                gd[f, here, cols] = green.astype(BF16)
                scaled_a[:, cols] = (green * weight).astype(BF16)
                rd[f, here, cols] = r32[lines, :].astype(BF16)

    def sum_tile(q):
        f, t = q // tiles, q % tiles
        here = pl.ds(pl.multiple_of(t * TILE, TILE), TILE)
        acc[...] += lax.dot_general(
            scaled_a[...], rd[f, here, :], (((0,), (0,)), ((), ())), preferred_element_type=F32
        )

    def forward(start, stop):
        def body(q, carry):
            shape_tile(q)
            sum_tile(q)
            return carry

        lax.fori_loop(start, stop, body, 0)

    def clear():
        acc[...] = jnp.zeros_like(acc)

    def squares(i, j):
        s_re = slice(i * lanes, (i + 1) * lanes)
        s_im = slice(half + i * lanes, half + (i + 1) * lanes)
        r_re = slice(j * lanes, (j + 1) * lanes)
        r_im = slice(half + j * lanes, half + (j + 1) * lanes)
        return s_re, s_im, r_re, r_im

    def finish_part(f):
        for k in range(pairs):
            s_re, s_im, r_re, r_im = squares(k // SIDE, k % SIDE)
            part[f, k, 0] = acc[s_re, r_re] - acc[s_im, r_im]
            part[f, k, 1] = acc[s_re, r_im] + acc[s_im, r_re]

    def remote(src, dst, send, recv, d):
        return pltpu.make_async_remote_copy(
            src_ref=src, dst_ref=dst, send_sem=send, recv_sem=recv,
            device_id={"slab": to(d)}, device_id_type=MESH,
        )

    def tab_copy(d, at):
        return remote(tab_send, tab_recv.at[at], tab_ss.at[d], tab_rs.at[d], d)

    def unit_copy(kind, d, at):
        return remote(
            unit_send.at[kind], unit_recv.at[kind, at], unit_ss.at[kind, d], unit_rs.at[kind, d], d
        )

    def obs_copy(d, at):
        return remote(obs_send.at[to(d)], obs_recv.at[at], obs_ss.at[d], obs_rs.at[d], d)

    def sum_copy(f, c, d, at):
        part_of = pl.ds(c * pairs, pairs)
        return remote(
            sum_send.at[f, to(d), part_of], sum_recv.at[f, at, part_of],
            sum_ss.at[f, c, d], sum_rs.at[f, c, d], d,
        )

    def use_copy(f, c, d, at):
        return remote(
            use_send.at[f, c, to(d)], adj.at[f, c, :, strip(at), :],
            use_ss.at[f, c, d], use_rs.at[f, c, d], d,
        )

    def ret_copy(d, at):
        return remote(ret_send.at[to(d)], ret_recv.at[at], ret_ss.at[d], ret_rs.at[d], d)

    def encode(kind, values, out):
        unit = unit_of(values)
        unit_send[kind] = unit
        gain = 1.0 / unit
        for at, value in enumerate(values):
            code = jnp.round(value * gain).astype(I16)
            out[:, at] = code.reshape(n, STRIP, lanes)

    fcks = [(f, c, k) for f in range(freqs) for c in range(2) for k in range(per)]

    def greet():
        for copy in tab_loads:
            copy.wait()
        lane = lax.broadcasted_iota(jnp.int32, tab_send.shape, 1)
        line = jnp.zeros(tab_send.shape, jnp.int32)
        for at, value in enumerate((st_ref[0, 0], st_ref[0, 1], rt_ref[0, 0], rt_ref[0, 1])):
            line = jnp.where(lane == at, value, line)
        tab_send[...] = line
        tab_recv[me] = line
        obs_load.wait()
        refl_load.wait()
        encode(freqs, [obs[f, k, c] for f, c, k in fcks], obs_send)
        pl.semaphore_wait(barrier, n)
        for d in order:
            tab_copy(d, me).start()
            unit_copy(freqs, d, me).start()
            obs_copy(d, me).start()

    def take_tables():
        for d in order:
            tab_copy(d, source(d)).wait_recv()
        copy = pltpu.make_async_copy(tab_recv, tab, tab_local)
        copy.start()
        copy.wait()

    def take_obs():
        for d in order:
            at = source(d)
            unit_copy(freqs, d, at).wait_recv()
            obs_copy(d, at).wait_recv()
            unit = unit_recv[freqs, at]
            for block, (f, c, k) in enumerate(fcks):
                obs_all[f, c, at * per + k] = obs_recv[at, block].astype(F32) * unit
        for f, c, k in fcks:
            obs_all[f, c, me * per + k] = obs[f, k, c, strip(me), :]

    def share(f):
        encode(f, [part[f, b, c] for c in range(2) for b in range(pairs)], sum_send.at[f])
        for d in order:
            unit_copy(f, d, me).start()
            sum_copy(f, 0, d, me).start()
        for d in order:
            sum_copy(f, 1, d, me).start()

    def tables():
        return [tuple(tab[s, 0, at] for at in range(4)) for s in range(n)]

    def reduce(f, c):
        for b in range(pairs):
            terms[me, b] = part[f, b, c, strip(me), :]
        for d in order:
            at = source(d)
            if c == 0:
                unit_copy(f, d, at).wait_recv()
            sum_copy(f, c, d, at).wait_recv()
            unit = unit_recv[f, at]
            for b in range(pairs):
                terms[at, b] = sum_recv[f, at, c * pairs + b].astype(F32) * unit
        rows_of, cols_of = [], []
        for table in tables():
            rows_of.append([
                jnp.where(table[0] == sb, 0, jnp.where(table[1] == sb, SIDE, pairs))
                for sb in range(panels // RB)
            ])
            cols_of.append([
                jnp.where(table[2] == rb, 0, jnp.where(table[3] == rb, 1, pairs)) for rb in range(RB)
            ])
        for panel in range(panels):
            value = -obs_all[f, c, panel]
            for s in range(n):
                index = jnp.minimum(rows_of[s][panel // RB] + cols_of[s][panel % RB], pairs)
                value = value + terms[s, index]
            res_all[f, c, panel] = value
            rounded[panel] = value.astype(BF16)
        for at, table in enumerate(tables()):
            for b in range(pairs):
                use_send[f, c, at, b] = rounded[table[b // SIDE] * RB + table[2 + b % SIDE]]
        for d in order:
            use_copy(f, c, d, me).start()
        for b in range(pairs):
            adj[f, c, b, strip(me), :] = use_send[f, c, me, b]

    def give_back():
        unit = unit_of([res_all[f, c, p] for f in range(freqs) for c in range(2) for p in range(panels)])
        unit_send[freqs + 1] = unit
        gain = 1.0 / unit
        for at in range(n):
            for block, (f, c, k) in enumerate(fcks):
                ret_send[at, block] = jnp.round(res_all[f, c, at * per + k] * gain).astype(I16)
        for d in order:
            unit_copy(freqs + 1, d, me).start()
            ret_copy(d, me).start()
        for d in order:
            tab_copy(d, me).wait_send()
            obs_copy(d, me).wait_send()
            for kind in range(freqs + 1):
                unit_copy(kind, d, me).wait_send()
            for f in range(freqs):
                for c in range(2):
                    sum_copy(f, c, d, me).wait_send()

    def take_back():
        for f, c, k in fcks:
            res_ref[f, k, c, strip(me), :] = res_all[f, c, me * per + k]
        for d in order:
            at = source(d)
            unit_copy(freqs + 1, d, at).wait_recv()
            ret_copy(d, at).wait_recv()
            unit = unit_recv[freqs + 1, at]
            for block, (f, c, k) in enumerate(fcks):
                res_ref[f, k, c, strip(at), :] = ret_recv[at, block].astype(F32) * unit

    def take_use(f, c):
        for d in order:
            use_copy(f, c, d, source(d)).wait_recv()

    def adjoint_terms(f, c, t):
        here = pl.ds(pl.multiple_of(t * SPAN, SPAN), SPAN)
        data = jnp.concatenate(
            [
                jnp.concatenate([adj[f, c, i * SIDE + j] for j in range(SIDE)], axis=1)
                for i in range(SIDE)
            ],
            axis=0,
        )
        by_re = jnp.dot(gd[f, here, :half], data, preferred_element_type=F32)
        by_im = jnp.dot(gd[f, here, half:], data, preferred_element_type=F32)
        rec_re = rd[f, here, :half].astype(F32)
        rec_im = rd[f, here, half:].astype(F32)
        if c == 0:
            terms = rec_re * by_re - rec_im * by_im
        else:
            terms = rec_re * by_im + rec_im * by_re
        result = terms[:, :lanes]
        for at in range(lanes, half, lanes):
            result = result + terms[:, at : at + lanes]
        return here, result

    def adjoint(f, c, turn):
        def body(t, carry):
            here, result = adjoint_terms(f, c, t)
            if turn > 0:
                result = total[here, :] + result
            if turn < 2 * freqs - 1:
                total[here, :] = result
                return carry
            sums = [
                jnp.sum(result[b * lanes : (b + 1) * lanes, :].T, axis=0, keepdims=True)
                for b in range(SPAN // lanes)
            ]
            summed[pl.ds(pl.multiple_of(t * SPAN // lanes, SPAN // lanes), SPAN // lanes), :] = jnp.concatenate(sums, 0)
            return carry

        lax.fori_loop(0, points // SPAN, body, 0)

    steps = {
        "greet": greet, "tables": take_tables, "take_obs": take_obs,
        "shape": shape_tile, "sum": sum_tile, "forward": forward, "clear": clear, "part": finish_part, "share": share, "reduce": reduce, "back": give_back,
        "use": take_use, "adjoint": adjoint,
    }
    for name, *rest in plan(tiles):
        steps[name](*rest)

    own_rows = grad_ref.shape[0]
    swap = pltpu.make_async_remote_copy(
        src_ref=summed.at[pl.ds(pl.multiple_of((1 - mine_f) * own_rows, own_rows), own_rows)],
        dst_ref=other,
        send_sem=ex_send,
        recv_sem=ex_recv,
        device_id={"freq": 1 - mine_f},
        device_id_type=MESH,
    )
    swap.start()

    for d in order:
        for f in range(freqs):
            for c in range(2):
                use_copy(f, c, d, me).wait_send()
    swap.wait()
    mine = summed[pl.ds(pl.multiple_of(mine_f * own_rows, own_rows), own_rows), :]
    grad_ref[...] = mine + other[...]
    grad_store = pltpu.make_async_copy(grad_ref, grad_hbm, out_sem.at[1])
    grad_store.start()
    take_back()
    res_store = pltpu.make_async_copy(res_ref, res_hbm, out_sem.at[0])
    res_store.start()
    for d in order:
        ret_copy(d, me).wait_send()
        unit_copy(freqs + 1, d, me).wait_send()
    grad_store.wait()
    res_store.wait()


def grid_plan(tiles):
    plan = [("greet",), ("clear",), ("forward", 0, tiles), ("part", 0), ("share", 0), ("clear",)]
    plan += [("forward", tiles, 2 * tiles), ("part", 1), ("share", 1), ("tables",), ("take_obs",)]
    plan += [
        ("reduce", 0, 0),
        ("reduce", 0, 1),
        ("reduce", 1, 0),
        ("use", 0, 0),
        ("adjoint", 0, 0, 0),
        ("reduce", 1, 1),
        ("back",),
        ("use", 0, 1),
        ("adjoint", 0, 1, 1),
        ("use", 1, 0),
        ("adjoint", 1, 0, 2),
        ("use", 1, 1),
        ("adjoint", 1, 1, 3),
    ]
    return plan


def ring_kernel(n, snake, st_ref, rt_ref, refl_ref, g_hbm, r_hbm, obs_ref, grad_ref, res_ref,
           raw, g32, r32, gd, rd, scaled, acc, part, first, held, gath_a, gath_b, gath_c, gath_d, adj, total, summed, other,
           raw_sem, rs_send, rs_recv, ag_send, ag_recv, ex_send, ex_recv):
    per = obs_ref.shape[1]
    lanes = obs_ref.shape[3]
    freqs, points, wide = gd.shape
    half = wide // 2
    tiles = points // TILE
    groups = TILE // lanes
    pairs = SIDE * SIDE
    gath = ((gath_a, gath_b), (gath_c, gath_d))
    me = lax.axis_index("slab")
    mine_f = lax.axis_index("freq")

    def index_of(pos):
        if not snake:
            return pos
        return 2 * pos + (pos // (n // 2)) * (2 * n - 1 - 4 * pos)

    place = me // 2 + (me % 2) * (n - 1 - 2 * (me // 2)) if snake else me
    ways = (1, -1)
    targets = tuple(index_of((place + way + n) % n) for way in ways)
    low = (n - 1) // 2
    high = n - 1 - low

    barrier = pltpu.get_barrier_semaphore()
    for target in targets:
        pl.semaphore_signal(barrier, inc=1, device_id={"slab": target}, device_id_type=MESH)
    pl.semaphore_signal(barrier, inc=1, device_id={"freq": 1 - mine_f}, device_id_type=MESH)

    def fetches(q, slot):
        return (
            pltpu.make_async_copy(g_hbm.at[q], raw.at[slot, 0], raw_sem.at[slot, 0]),
            pltpu.make_async_copy(r_hbm.at[q], raw.at[slot, 1], raw_sem.at[slot, 1]),
        )

    for q in range(2):
        for copy in fetches(q, q):
            copy.start()

    def forward_tile(f, t):
        q = f * tiles + t
        slot = q % 2
        for copy in fetches(q, slot):
            copy.wait()
        g32[...] = raw[slot, 0].astype(F32)
        r32[...] = raw[slot, 1].astype(F32)

        @pl.when(q + 2 < freqs * tiles)
        def _():
            for copy in fetches(q + 2, slot):
                copy.start()

        refl = refl_ref[pl.ds(pl.multiple_of(t * groups, groups), groups), :]
        weight = jnp.concatenate(
            [jnp.broadcast_to(refl[b : b + 1, :], (lanes, lanes)).T for b in range(groups)], axis=0
        )
        here = pl.ds(pl.multiple_of(t * TILE, TILE), TILE)
        for block in range(SIDE):
            for comp in range(2):
                rows = pl.ds(block * 2 + comp, TILE, stride=2 * SIDE)
                cols = slice(comp * half + block * lanes, comp * half + (block + 1) * lanes)
                green = g32[rows, :]
                gd[f, here, cols] = green.astype(BF16)
                scaled[:, cols] = (green * weight).astype(BF16)
                rd[f, here, cols] = r32[rows, :].astype(BF16)
        prod = lax.dot_general(
            scaled[...], rd[f, here, :], (((0,), (0,)), ((), ())), preferred_element_type=F32
        )
        acc[...] += prod

    def forward(f, start, stop):
        def body(t, carry):
            forward_tile(f, t)
            return carry

        lax.fori_loop(start, stop, body, 0)

    def squares(i, j):
        s_re = slice(i * lanes, (i + 1) * lanes)
        s_im = slice(half + i * lanes, half + (i + 1) * lanes)
        r_re = slice(j * lanes, (j + 1) * lanes)
        r_im = slice(half + j * lanes, half + (j + 1) * lanes)
        return s_re, s_im, r_re, r_im

    def finish_part(f):
        for k in range(pairs):
            s_re, s_im, r_re, r_im = squares(k // SIDE, k % SIDE)
            part[f, k, 0] = acc[s_re, r_re] - acc[s_im, r_im]
            part[f, k, 1] = acc[s_re, r_im] + acc[s_im, r_re]
        part[f, pairs] = jnp.zeros((2, lanes, lanes), F32)

    def hops(f, w):
        return high if f == w else low

    lanes_of = [(c, w) for c in range(2) for w in range(2)]

    def held_at(panel):
        sb = panel // RB
        rb = panel % RB
        i = jnp.where(st_ref[0, 0] == sb, 0, jnp.where(st_ref[0, 1] == sb, SIDE, 2 * pairs))
        j = jnp.where(rt_ref[0, 0] == rb, 0, jnp.where(rt_ref[0, 1] == rb, 1, 2 * pairs))
        return jnp.minimum(i + j, pairs)

    def own(f, c, w, away):
        owner = index_of((place + ways[w] * away + n) % n)
        return [part[f, held_at(owner * per + k), c] for k in range(per)]

    def rs_copy(f, c, w, src, step):
        return pltpu.make_async_remote_copy(
            src_ref=src,
            dst_ref=held.at[f, c, w, step],
            send_sem=rs_send.at[f, c, w, step],
            recv_sem=rs_recv.at[f, c, w, step],
            device_id={"slab": targets[w]},
            device_id_type=MESH,
        )

    def ag_copy(f, c, w, step, away):
        owner = index_of((place - ways[w] * away + n) % n)
        view = gath[f][c].at[pl.ds(owner * per, per)]
        return pltpu.make_async_remote_copy(
            src_ref=view,
            dst_ref=view,
            send_sem=ag_send.at[f, c, w, step],
            recv_sem=ag_recv.at[f, c, w, step],
            device_id={"slab": targets[w]},
            device_id_type=MESH,
        )

    def rs_start(f):
        for c, w in lanes_of:
            mine = own(f, c, w, hops(f, w))
            for k in range(per):
                first[f, c, w, k] = mine[k]
            rs_copy(f, c, w, first.at[f, c, w], 0).start()

    def rs_pass(f, step, only=None):
        for c, w in lanes_of:
            if only is not None and w != only:
                continue
            rs_copy(f, c, w, held.at[f, c, w, step], step).wait_recv()
            mine = own(f, c, w, hops(f, w) - step - 1)
            for k in range(per):
                held[f, c, w, step, k] = held[f, c, w, step, k] + mine[k]
            rs_copy(f, c, w, held.at[f, c, w, step], step + 1).start()

    def ag_pass(f, step, only=None):
        for c, w in lanes_of:
            if only is not None and w != only:
                continue
            ag_copy(f, c, w, step, step + 1).wait_recv()
            ag_copy(f, c, w, step + 1, step + 1).start()

    def rs_longer(f):
        if high > low:
            rs_pass(f, high - 2, f)

    def ag_longer(f):
        if high > low:
            ag_pass(f, high - 2, f)

    def rs_finish(f):
        for c in range(2):
            for w in range(2):
                last = hops(f, w) - 1
                rs_copy(f, c, w, held.at[f, c, w, last], last).wait_recv()
            mine = own(f, c, 0, 0)
            for k in range(per):
                value = (
                    held[f, c, 0, hops(f, 0) - 1, k] + held[f, c, 1, hops(f, 1) - 1, k] + mine[k]
                ) - obs_ref[f, k, c]
                res_ref[f, k, c] = value
                gath[f][c][me * per + k] = value.astype(BF16)
            for w in range(2):
                ag_copy(f, c, w, 0, 0).start()

    def ag_finish(f, c):
        for w in range(2):
            last = hops(f, w) - 1
            ag_copy(f, c, w, last, last + 1).wait_recv()
        for k in range(pairs):
            i, j = k // SIDE, k % SIDE
            panel = st_ref[0, i] * RB + rt_ref[0, j]
            s_re, s_im, r_re, r_im = squares(i, j)
            adj[f, c, s_re, r_re] = gath[f][c][panel]

    def adjoint_terms(f, c, t):
        here = pl.ds(pl.multiple_of(t * TILE, TILE), TILE)
        data = adj[f, c]
        by_re = jnp.dot(gd[f, here, :half], data, preferred_element_type=F32)
        by_im = jnp.dot(gd[f, here, half:], data, preferred_element_type=F32)
        rec_re = rd[f, here, :half].astype(F32)
        rec_im = rd[f, here, half:].astype(F32)
        if c == 0:
            terms = rec_re * by_re - rec_im * by_im
        else:
            terms = rec_re * by_im + rec_im * by_re
        result = terms[:, :lanes]
        for at in range(lanes, half, lanes):
            result = result + terms[:, at : at + lanes]
        return here, result

    def adjoint(f, c):
        def body(t, carry):
            here, result = adjoint_terms(f, c, t)
            if f + c > 0:
                result = total[here, :] + result
            if f + c < 2:
                total[here, :] = result
                return carry
            rows = [
                jnp.sum(result[b * lanes : (b + 1) * lanes, :].T, axis=0, keepdims=True)
                for b in range(groups)
            ]
            summed[pl.ds(pl.multiple_of(t * groups, groups), groups), :] = jnp.concatenate(rows, 0)
            return carry

        lax.fori_loop(0, tiles, body, 0)

    acc[...] = jnp.zeros_like(acc)
    forward(0, 0, tiles)
    finish_part(0)
    pl.semaphore_wait(barrier, 3)
    rs_start(0)
    acc[...] = jnp.zeros_like(acc)
    forward(1, 0, tiles // 2)
    rs_pass(0, 0)
    forward(1, tiles // 2, tiles)
    finish_part(1)
    rs_start(1)

    def rs_both(step, carry):
        rs_pass(0, step)
        rs_pass(1, step - 1)
        return carry

    lax.fori_loop(1, low - 1, rs_both, 0)
    rs_longer(0)
    rs_pass(1, low - 2)
    rs_finish(0)
    rs_longer(1)
    ag_pass(0, 0)
    rs_finish(1)

    def ag_both(step, carry):
        ag_pass(0, step)
        ag_pass(1, step - 1)
        return carry

    lax.fori_loop(1, low - 1, ag_both, 0)
    ag_longer(0)
    ag_pass(1, low - 2)
    ag_finish(0, 0)
    adjoint(0, 0)
    ag_longer(1)
    ag_finish(0, 1)
    adjoint(0, 1)
    ag_finish(1, 0)
    adjoint(1, 0)
    ag_finish(1, 1)
    adjoint(1, 1)

    own_rows = grad_ref.shape[0]
    swap = pltpu.make_async_remote_copy(
        src_ref=summed.at[pl.ds(pl.multiple_of((1 - mine_f) * own_rows, own_rows), own_rows)],
        dst_ref=other,
        send_sem=ex_send,
        recv_sem=ex_recv,
        device_id={"freq": 1 - mine_f},
        device_id_type=MESH,
    )
    swap.start()

    def drain(step, carry):
        for f in range(2):
            for c, w in lanes_of:
                rs_copy(f, c, w, first.at[f, c, w], step).wait_send()
                ag_copy(f, c, w, step, step).wait_send()
        return carry

    lax.fori_loop(0, low, drain, 0)
    if high > low:
        for f in range(2):
            for c in range(2):
                rs_copy(f, c, f, first.at[f, c, f], high - 1).wait_send()
                ag_copy(f, c, f, high - 1, high - 1).wait_send()
    swap.wait()
    mine = summed[pl.ds(pl.multiple_of(mine_f * own_rows, own_rows), own_rows), :]
    grad_ref[...] = mine + other[...]


def interleaved_tiles(green, lanes):
    freqs, points, comps, width = green.shape
    view = green.reshape(freqs, points, comps, width // lanes, lanes).transpose(0, 1, 3, 2, 4)
    tiles = freqs * points // TILE
    return view.reshape(tiles, TILE * comps * width // lanes, lanes)


def grid_on_device(reflectivity, source_green, receiver_green, observed, source_table, receiver_table):
    freqs, points, comps, width = source_green.shape
    per = observed.shape[1]
    lanes = observed.shape[3]
    pairs = SIDE * SIDE
    n = lanes // STRIP
    panels = n * per
    blocks = 2 * pairs
    wide = comps * width
    tall = TILE * wide // lanes
    lines = points // lanes
    vmem = pl.BlockSpec(memory_space=pltpu.VMEM)
    smem = pl.BlockSpec(memory_space=pltpu.SMEM)
    hbm = pl.BlockSpec(memory_space=pl.ANY)
    sem = pltpu.SemaphoreType.DMA

    def codes(*shape):
        return pltpu.VMEM(shape + (STRIP, lanes), I16)

    gradient, residual = pl.pallas_call(
        functools.partial(grid_kernel, grid_plan),
        in_specs=[hbm, hbm, hbm, hbm, hbm, hbm],
        out_specs=[hbm, hbm],
        out_shape=[
            jax.ShapeDtypeStruct((lines // 2, lanes), F32),
            jax.ShapeDtypeStruct(observed.shape, F32),
        ],
        scratch_shapes=[
            pltpu.SMEM(source_table.shape, jnp.int32),
            pltpu.SMEM(receiver_table.shape, jnp.int32),
            pltpu.VMEM((lines // 2, lanes), F32),
            pltpu.VMEM(observed.shape, F32),
            sem((2,)),
            pltpu.VMEM(observed.shape, F32),
            pltpu.VMEM((lines, lanes), F32),
            pltpu.VMEM((2, 2, tall, lanes), BF16),
            pltpu.VMEM((tall, lanes), F32),
            pltpu.VMEM((tall, lanes), F32),
            pltpu.VMEM((freqs, points, wide), BF16),
            pltpu.VMEM((freqs, points, wide), BF16),
            pltpu.VMEM((TILE, wide), BF16),
            pltpu.VMEM((wide, wide), F32),
            pltpu.VMEM((freqs, pairs, 2, lanes, lanes), F32),
            pltpu.VMEM((freqs, 2, pairs, lanes, lanes), BF16),
            pltpu.VMEM((points, lanes), F32),
            pltpu.VMEM((lines, lanes), F32),
            pltpu.VMEM((lines // 2, lanes), F32),
            pltpu.VMEM((8, 128), jnp.int32),
            pltpu.VMEM((n, 8, 128), jnp.int32),
            pltpu.SMEM((n, 8, 128), jnp.int32),
            pltpu.VMEM((freqs + 2, 1, lanes), F32),
            pltpu.VMEM((freqs + 2, n, 1, lanes), F32),
            codes(n, blocks), codes(n, blocks),
            pltpu.VMEM((freqs, 2, panels, STRIP, lanes), F32),
            codes(freqs, n, blocks), codes(freqs, n, blocks),
            pltpu.VMEM((n, pairs + 1, STRIP, lanes), F32),
            pltpu.VMEM((freqs, 2, panels, STRIP, lanes), F32),
            pltpu.VMEM((panels, STRIP, lanes), BF16),
            pltpu.VMEM((freqs, 2, n, pairs, STRIP, lanes), BF16),
            codes(n, blocks), codes(n, blocks),
            sem((4,)),
            sem((2, 2)),
            sem((freqs + 2, n)), sem((freqs + 2, n)),
            sem((n,)), sem((n,)), sem,
            sem((n,)), sem((n,)),
            sem((freqs, 2, n)), sem((freqs, 2, n)),
            sem((freqs, 2, n)), sem((freqs, 2, n)),
            sem((n,)), sem((n,)),
            sem, sem,
        ],
        compiler_params=pltpu.CompilerParams(
            collective_id=0, has_side_effects=True, vmem_limit_bytes=VMEM_BYTES
        ),
        name="migration",
    )(
        source_table,
        receiver_table,
        reflectivity.reshape(lines, lanes),
        interleaved_tiles(source_green, lanes),
        interleaved_tiles(receiver_green, lanes),
        observed,
    )
    gradient, residual = pl.pallas_call(
        hand_over,
        in_specs=[vmem, vmem],
        out_specs=[hbm, hbm],
        out_shape=[
            jax.ShapeDtypeStruct(gradient.shape, F32),
            jax.ShapeDtypeStruct(residual.shape, F32),
        ],
        scratch_shapes=[sem((2,))],
        name="hand_over",
    )(gradient, residual)
    return gradient.reshape(points // 2), residual


def ring_on_device(reflectivity, source_green, receiver_green, observed, source_table, receiver_table):
    freqs, points, comps, width = source_green.shape
    per = observed.shape[1]
    lanes = observed.shape[3]
    n = lax.axis_size("slab")
    pairs = SIDE * SIDE
    wide = comps * width
    tall = TILE * wide // lanes
    rows = points // lanes
    vmem = pl.BlockSpec(memory_space=pltpu.VMEM)
    smem = pl.BlockSpec(memory_space=pltpu.SMEM)
    hbm = pl.BlockSpec(memory_space=pl.ANY)
    hop_sems = pltpu.SemaphoreType.DMA((freqs, 2, 2, n // 2))
    gradient, residual = pl.pallas_call(
        functools.partial(ring_kernel, n, n == 8),
        in_specs=[smem, smem, vmem, hbm, hbm, vmem],
        out_specs=[vmem, vmem],
        out_shape=[
            jax.ShapeDtypeStruct((rows // 2, lanes), F32),
            jax.ShapeDtypeStruct(observed.shape, F32),
        ],
        scratch_shapes=[
            pltpu.VMEM((2, 2, tall, lanes), BF16),
            pltpu.VMEM((tall, lanes), F32),
            pltpu.VMEM((tall, lanes), F32),
            pltpu.VMEM((freqs, points, wide), BF16),
            pltpu.VMEM((freqs, points, wide), BF16),
            pltpu.VMEM((TILE, wide), BF16),
            pltpu.VMEM((wide, wide), F32),
            pltpu.VMEM((freqs, pairs + 1, 2, lanes, lanes), F32),
            pltpu.VMEM((freqs, 2, 2, per, lanes, lanes), F32),
            pltpu.VMEM((freqs, 2, 2, n // 2, per, lanes, lanes), F32),
            pltpu.VMEM((n * per, lanes, lanes), BF16),
            pltpu.VMEM((n * per, lanes, lanes), BF16),
            pltpu.VMEM((n * per, lanes, lanes), BF16),
            pltpu.VMEM((n * per, lanes, lanes), BF16),
            pltpu.VMEM((freqs, 2, width, width), BF16),
            pltpu.VMEM((points, lanes), F32),
            pltpu.VMEM((rows, lanes), F32),
            pltpu.VMEM((rows // 2, lanes), F32),
            pltpu.SemaphoreType.DMA((2, 2)),
            hop_sems,
            hop_sems,
            hop_sems,
            hop_sems,
            pltpu.SemaphoreType.DMA,
            pltpu.SemaphoreType.DMA,
        ],
        compiler_params=pltpu.CompilerParams(collective_id=0, has_side_effects=True, vmem_limit_bytes=VMEM_BYTES),
        name="migration",
    )(
        source_table,
        receiver_table,
        reflectivity.reshape(rows, lanes),
        interleaved_tiles(source_green, lanes),
        interleaved_tiles(receiver_green, lanes),
        observed,
    )
    return gradient.reshape(points // 2), residual


def solution(mesh):
    on_device = grid_on_device if mesh.shape["slab"] == SLICES else ring_on_device
    return jax.shard_map(
        on_device,
        mesh=mesh,
        in_specs=(
            P(("parts", "slab")),
            P("freq", ("parts", "slab"), None, None),
            P("freq", ("parts", "slab"), None, None),
            P("freq", ("parts", "slab"), None, None, None),
            P(("parts", "slab"), None),
            P(("parts", "slab"), None),
        ),
        out_specs=(P(("parts", "slab", "freq")), P("freq", ("parts", "slab"), None, None, None)),
        check_vma=False,
    )
```
